256 devices in a mesh: dp: 16 (over z, core), filter: 16 (over x, y).
Axes of the slice: x: 4, y: 4, z: 8, core: 2. Of those that a mesh axis runs over, the one named last changes fastest.
Arguments:
- patches: bfloat16 [256, 48, 2048], P('filter', 'dp'), may hold values from -6 to 6
- cotangent: bfloat16 [256, 48, 2048], P('filter', 'dp'), may hold values from -6 to 6
- first_weight: bfloat16 [27, 256, 256], P(None, 'filter'), may hold values from -0.078125 to 0.078125
- second_weight: bfloat16 [27, 256, 256], P(None, 'filter'), may hold values from -0.078125 to 0.078125
- counts: int32 [16], P('dp'), may hold values from 0 to 3, as said below
Outputs:
- output_maps: float32 [256, 48, 2048], P('filter', 'dp')
- input_grad: float32 [256, 48, 2048], P('filter', 'dp')
- first_grad: float32 [27, 256, 256], P(None, 'filter')
- second_grad: float32 [27, 256, 256], P(None, 'filter')
The draws below stay inside these ranges and needn't reach their ends.
Inputs may be any that keep to these rules, and one draw needn't show every extreme that they name: The counts of all groups sum to 16; one group holds exactly 3 live patches. Live patches of a group occupy its first slots.
All inputs are finite; a program needn't handle non-finite values.
Results may differ from the reference program's by a relative error of at most 0.0029.
Values may be sent and summed in bfloat16 or wider, within the bound.
No kernel may reach another device: no remote copies, remote signals or barrier semaphores. Data moves between devices by JAX's collectives and lax.ppermute only.
A program may use at most 128 MiB of HBM per device.

```python
import jax
import jax.numpy as jnp
from jax import lax

C = 256
PX = 8
PY = 16
PZ = 16
CAP = 3
CELLS = 2048
SLOTS = 48
N_DP = 16


def draw_counts(key, part):
    order = jax.random.permutation(key, N_DP)
    counts = jnp.ones((N_DP,), jnp.int32)
    counts = counts.at[order[0]].set(CAP).at[order[1]].set(0).at[order[2]].set(0)
    pairs = (N_DP - 3) // 2
    if pairs > 0:
        flips = jax.random.randint(jax.random.fold_in(key, 1), (pairs,), 0, 2).astype(jnp.int32)
        counts = counts.at[order[3:3 + 2 * pairs:2]].add(flips)
        counts = counts.at[order[4:4 + 2 * pairs:2]].add(-flips)
    return counts


def block_scale(rng, extent, split, low, top_value):
    def one(axis_at, blocks):
        draws = jax.random.uniform(jax.random.fold_in(jax.random.fold_in(rng, 6), axis_at), (blocks,), jnp.float32, low / len(split), top_value / len(split))
        return jnp.repeat(jnp.exp(draws), extent[axis_at] // blocks).reshape((-1,) + (1,) * (len(extent) - axis_at - 1))

    loudness = one(*split[0])
    for cut in split[1:]:
        loudness = loudness * one(*cut)
    return loudness


def gaussian(rng, extent, scale, most, pieces=(), kind=jnp.bfloat16):
    level = block_scale(rng, extent, pieces, -0.22, 0.18) if pieces else 1.0
    values = jax.random.normal(rng, extent, jnp.float32) * scale * level
    return jnp.minimum(jnp.maximum(values, -most), most).astype(kind)


def setup_inputs(seed: int = 0) -> dict:
    arg_keys = jax.random.split(jax.random.key(seed), 6)
    return {
        "patches": gaussian(arg_keys[0], (C, SLOTS, CELLS), 1.0, 6.0, ((0, 16), (1, 16))),
        "cotangent": gaussian(arg_keys[1], (C, SLOTS, CELLS), 1.0, 6.0, ((0, 16), (1, 16))),
        "first_weight": gaussian(arg_keys[2], (27, C, C), (27 * C) ** -0.5, 0.078125, ((1, 16),)),
        "second_weight": gaussian(arg_keys[3], (27, C, C), (27 * C) ** -0.5, 0.078125, ((1, 16),)),
        "counts": draw_counts(jax.random.fold_in(arg_keys[5], 71), 0),
    }


stencil_taps = [(ox, oy, oz) for ox in (-1, 0, 1) for oy in (-1, 0, 1) for oz in (-1, 0, 1)]

def shift_cells(value, ox, oy, oz):
    span = PY * PZ + PZ + 1
    step = ox * PY * PZ + oy * PZ + oz
    padded = jnp.pad(value, [(0, 0)] * (value.ndim - 1) + [(span, span)])
    moved = lax.slice_in_dim(padded, span + step, span + step + CELLS, axis=value.ndim - 1)
    cell = jnp.arange(CELLS, dtype=jnp.int32)
    pos_x = cell // (PY * PZ) + ox
    pos_y = cell // PZ % PY + oy
    pos_z = cell % PZ + oz
    inside = (pos_x >= 0) & (pos_x < PX) & (pos_y >= 0) & (pos_y < PY) & (pos_z >= 0) & (pos_z < PZ)
    return jnp.where(inside, moved, jnp.zeros_like(moved))

def shifted_stack(value):
    return jnp.stack([shift_cells(value, -ox, -oy, -oz) for ox, oy, oz in stencil_taps])

def forward_conv(inputs, weight):
    proj = jnp.einsum('toi,isc->tosc', weight.astype(jnp.float32), inputs.astype(jnp.float32))
    total = jnp.zeros(proj.shape[1:], jnp.float32)
    for t, (ox, oy, oz) in enumerate(stencil_taps):
        total = total + shift_cells(proj[t], ox, oy, oz)
    return total

def backward_conv(grads, weight):
    stack = shifted_stack(grads).astype(jnp.float32)
    return jnp.einsum('toi,tosc->isc', weight.astype(jnp.float32), stack)

def weight_conv(grads, inputs):
    stack = shifted_stack(grads).astype(jnp.float32)
    return jnp.einsum('tosc,isc->toi', stack, inputs.astype(jnp.float32))

def reference(patches, cotangent, first_weight, second_weight, counts):
    live = (jnp.arange(CAP, dtype=jnp.int32)[None, :] < counts[:, None]).reshape(SLOTS)
    xs = jnp.moveaxis(patches, 1, 0)[:, :, None, :]
    gs = jnp.moveaxis(cotangent, 1, 0)[:, :, None, :]

    def one_slot(carry, item):
        acc_one, acc_two = carry
        inputs, grads, alive = item
        gate = jnp.where(alive, 1.0, 0.0).astype(jnp.float32)
        masked = (grads.astype(jnp.float32) * gate).astype(jnp.bfloat16)
        first = forward_conv(inputs, first_weight)
        hidden = jax.nn.silu(first).astype(jnp.bfloat16)
        out = forward_conv(hidden, second_weight) * gate
        hidden_grad = backward_conv(masked, second_weight)
        sg = jax.nn.sigmoid(first)
        delta = (hidden_grad * sg * (1.0 + first * (1.0 - sg))).astype(jnp.bfloat16)
        in_grad = backward_conv(delta, first_weight)
        acc_two = acc_two + weight_conv(masked, hidden)
        acc_one = acc_one + weight_conv(delta, inputs)
        return ((acc_one, acc_two), (out, in_grad))
    zeros = jnp.zeros((27, C, C), jnp.float32)
    (acc_one, acc_two), (outs, grads_in) = lax.scan(one_slot, (zeros, zeros), (xs, gs, live))
    scale = 1.0 / jnp.sqrt(jnp.float32(N_DP * CELLS))
    output_maps = jnp.moveaxis(outs[:, :, 0, :], 0, 1)
    input_grad = jnp.moveaxis(grads_in[:, :, 0, :], 0, 1)
    return (output_maps, input_grad, acc_one * scale, acc_two * scale)
```

```python
import functools

import jax
import jax.numpy as jnp
from jax import lax
from jax.experimental import pallas as pl
from jax.experimental.pallas import tpu as pltpu
from jax.sharding import PartitionSpec as P

PX = 8
PY = 16
PZ = 16
CAP = 3
CELLS = 2048
PLANE = PY * PZ
C = 256
BLK = 16
TAPS = 27
ROWS = TAPS * BLK

SIDE = 4


def axis_masks():
    cell = lax.broadcasted_iota(jnp.int32, (BLK, CELLS), 1)
    pos_y = (cell >> 4) & 15
    pos_z = cell & 15
    in_y = {-1: pos_y > 0, 0: None, 1: pos_y < PY - 1}
    in_z = {-1: pos_z > 0, 0: None, 1: pos_z < PZ - 1}
    return in_y, in_z


def shift_x(v, ox):
    if ox == 0:
        return v
    zero = jnp.zeros((v.shape[0], PLANE), v.dtype)
    if ox > 0:
        return jnp.concatenate([v[:, PLANE:], zero], axis=1)
    return jnp.concatenate([zero, v[:, :-PLANE]], axis=1)


def shift_yz(v, oy, oz, masks):
    step = oy * PZ + oz
    if step == 0:
        return v
    v = pltpu.roll(v, (-step) % CELLS, 1)
    for inside in (masks[0][oy], masks[1][oz]):
        if inside is not None:
            v = jnp.where(inside, v, 0.0)
    return v


def tap_conv(w_ref, full, sign, masks):
    proj = [
        jnp.dot(w_ref[k * 9 * BLK:(k + 1) * 9 * BLK, :], full, preferred_element_type=jnp.float32)
        for k in range(3)
    ]
    total = None
    for oy in (-1, 0, 1):
        for oz in (-1, 0, 1):
            at = (3 * (oy + 1) + oz + 1) * BLK
            part = None
            for ox in (-1, 0, 1):
                term = shift_x(proj[ox + 1][at:at + BLK, :], sign * ox)
                part = term if part is None else part + term
            part = shift_yz(part, sign * oy, sign * oz, masks)
            total = part if total is None else total + part
    return total


def tap_stack(stack_ref, v, sign, masks):
    for oy in (-1, 0, 1):
        for oz in (-1, 0, 1):
            moved = shift_yz(v, sign * oy, sign * oz, masks)
            for ox in (-1, 0, 1):
                t = 9 * (ox + 1) + 3 * (oy + 1) + (oz + 1)
                stack_ref[t * BLK:(t + 1) * BLK, :] = shift_x(moved, sign * ox).astype(jnp.bfloat16)


def place(scalars, pieces, full_ref, outer_is_x):
    x, y = scalars[1], scalars[2]
    for outer in range(SIDE):
        for half in range(2):
            for k in range(2):
                inner = 2 * half + k
                dx, dy = (outer, inner) if outer_is_x else (inner, outer)
                block = lax.rem(x + dx, SIDE) * SIDE + lax.rem(y + dy, SIDE)
                at = pl.multiple_of(block * BLK, BLK)
                full_ref[pl.ds(at, BLK), :] = pieces[2 * outer + half][k, 0]


def over_cells(a, b):
    return lax.dot_general(a, b, (((1,), (1,)), ((), ())), preferred_element_type=jnp.float32)


def kernel_one(scalars, *refs):
    px, gx = refs[0:8], refs[8:16]
    w1, w2t, hid_out, del_out, grad_out, full_p, full_g, stack = refs[16:]
    s = pl.program_id(0)

    @pl.when(s == 0)
    def _():
        grad_out[...] = jnp.zeros_like(grad_out)

    @pl.when(s >= scalars[0])
    def _():
        hid_out[...] = jnp.zeros_like(hid_out)
        del_out[...] = jnp.zeros_like(del_out)

    @pl.when(s < scalars[0])
    def _():
        masks = axis_masks()
        place(scalars, px, full_p, True)
        place(scalars, gx, full_g, False)
        first = tap_conv(w1, full_p[...], 1, masks)
        hidden_grad = tap_conv(w2t, full_g[...], -1, masks)
        sigma = 1.0 / (1.0 + jnp.exp(-first))
        hidden = (first * sigma).astype(jnp.bfloat16)
        delta = (hidden_grad * sigma * (1.0 + first * (1.0 - sigma))).astype(jnp.bfloat16)
        hid_out[0] = hidden
        del_out[0] = delta
        tap_stack(stack, delta.astype(jnp.float32), -1, masks)
        grad_out[:, 0] += over_cells(full_p[...], stack[...]).reshape(BLK, BLK, ROWS)
        tap_stack(stack, hidden.astype(jnp.float32), 1, masks)
        grad_out[:, 1] += over_cells(full_g[...], stack[...]).reshape(BLK, BLK, ROWS)


def kernel_two(scalars, *refs):
    hx, dx = refs[0:8], refs[8:16]
    w2, w1t, out_ref, in_ref, full_h, full_d = refs[16:]
    s = pl.program_id(0)

    @pl.when(s >= scalars[0])
    def _():
        out_ref[...] = jnp.zeros_like(out_ref)
        in_ref[...] = jnp.zeros_like(in_ref)

    @pl.when(s < scalars[0])
    def _():
        masks = axis_masks()
        place(scalars, hx, full_h, True)
        place(scalars, dx, full_d, False)
        out_ref[0] = tap_conv(w2, full_h[...], 1, masks)
        in_ref[0] = tap_conv(w1t, full_d[...], -1, masks)


def from_x(step):
    return [(((x + step) % SIDE) * SIDE + y, x * SIDE + y) for x in range(SIDE) for y in range(SIDE)]


def from_y(step):
    return [(x * SIDE + (y + step) % SIDE, x * SIDE + y) for x in range(SIDE) for y in range(SIDE)]


def gather(v, inner, outer):
    move = lambda a, pairs: lax.ppermute(a, "filter", pairs)
    near = [v] + [move(v, inner(k)) for k in (1, 2, 3)]
    own = [jnp.stack(near[:2]), jnp.stack(near[2:])]
    ahead = [move(h, outer(1)) for h in own]
    behind = [move(h, outer(3)) for h in own]
    across = [move(ahead[0], outer(1)), move(behind[1], outer(3))]
    return own + ahead + across + behind


def specs_of(count):
    piece = pl.BlockSpec((2, 1, BLK, CELLS), lambda s, *_: (0, s, 0, 0))
    weight = pl.BlockSpec((ROWS, C), lambda s, *_: (0, 0))
    return [piece] * count + [weight] * 2


def slot_spec():
    return pl.BlockSpec((1, BLK, CELLS), lambda s, *_: (s, 0, 0))


def call_one(scalars, pieces, w1, w2t):
    slots = pieces[0].shape[1]
    flat = jax.ShapeDtypeStruct((slots, BLK, CELLS), jnp.bfloat16)
    return pl.pallas_call(
        kernel_one,
        name="layer_one",
        grid_spec=pltpu.PrefetchScalarGridSpec(
            num_scalar_prefetch=1,
            grid=(slots,),
            in_specs=specs_of(16),
            out_specs=[
                slot_spec(),
                slot_spec(),
                pl.BlockSpec((BLK, 2, BLK, ROWS), lambda s, *_: (0, 0, 0, 0)),
            ],
            scratch_shapes=[
                pltpu.VMEM((C, CELLS), jnp.bfloat16),
                pltpu.VMEM((C, CELLS), jnp.bfloat16),
                pltpu.VMEM((ROWS, CELLS), jnp.bfloat16),
            ],
        ),
        out_shape=[flat, flat, jax.ShapeDtypeStruct((BLK, 2, BLK, ROWS), jnp.float32)],
        compiler_params=pltpu.CompilerParams(vmem_limit_bytes=48 * 1024 * 1024),
        cost_estimate=pl.CostEstimate(
            flops=slots * 8 * ROWS * C * CELLS, transcendentals=slots * BLK * CELLS, bytes_accessed=slots * 4 * C * CELLS
        ),
    )(scalars, *pieces, w1, w2t)


def call_two(scalars, pieces, w2, w1t):
    slots = pieces[0].shape[1]
    flat = jax.ShapeDtypeStruct((slots, BLK, CELLS), jnp.float32)
    return pl.pallas_call(
        kernel_two,
        name="layer_two",
        grid_spec=pltpu.PrefetchScalarGridSpec(
            num_scalar_prefetch=1,
            grid=(slots,),
            in_specs=specs_of(16),
            out_specs=[slot_spec(), slot_spec()],
            scratch_shapes=[
                pltpu.VMEM((C, CELLS), jnp.bfloat16),
                pltpu.VMEM((C, CELLS), jnp.bfloat16),
            ],
        ),
        out_shape=[flat, flat],
        compiler_params=pltpu.CompilerParams(vmem_limit_bytes=48 * 1024 * 1024),
        cost_estimate=pl.CostEstimate(
            flops=slots * 4 * ROWS * C * CELLS, transcendentals=0, bytes_accessed=slots * 4 * C * CELLS
        ),
    )(scalars, *pieces, w2, w1t)


def by_input_channel(w):
    return w.reshape(TAPS, BLK, BLK, BLK).transpose(2, 1, 0, 3).reshape(BLK, BLK, ROWS)


def shards(patches, cotangent, first_weight, second_weight, counts):
    me = lax.axis_index("filter")
    scalars = jnp.stack([counts[0], me // SIDE, me % SIDE]).astype(jnp.int32)
    p = patches.transpose(1, 0, 2)
    g = cotangent.transpose(1, 0, 2)
    all_p = gather(p, from_y, from_x)
    all_g = gather(g, from_x, from_y)

    sent = jnp.stack([by_input_channel(first_weight), by_input_channel(second_weight)], axis=1)
    turned = lax.all_to_all(sent, "filter", 0, 0, tiled=True)
    w1t = turned[:, 0].reshape(C, ROWS).T
    w2t = turned[:, 1].reshape(C, ROWS).T
    w1 = first_weight.reshape(ROWS, C)
    w2 = second_weight.reshape(ROWS, C)

    hidden, delta, grads = call_one(scalars, all_p + all_g, w1, w2t)

    parts = lax.all_to_all(grads, "dp", 0, 0, tiled=True)
    scale = 1.0 / jnp.sqrt(jnp.float32(lax.axis_size("dp") * CELLS))
    mine = parts.sum(axis=0) * scale
    swap = [(d * BLK + f, f * BLK + d) for d in range(BLK) for f in range(BLK)]
    second = lax.ppermute(mine[1], ("dp", "filter"), swap)
    second = second.reshape(BLK, TAPS, BLK).transpose(2, 1, 0).reshape(BLK, ROWS)
    pair = jnp.stack([mine[0], second])
    whole = lax.all_gather(pair, "dp", axis=0)
    whole = whole.transpose(1, 3, 0, 2).reshape(2, TAPS, BLK, C)

    all_h = gather(hidden, from_y, from_x)
    all_d = gather(delta, from_x, from_y)
    out, in_grad = call_two(scalars, all_h + all_d, w2, w1t)
    return (out.transpose(1, 0, 2), in_grad.transpose(1, 0, 2), whole[0], whole[1])


def solution(mesh):
    placed = (
        P("filter", "dp", None),
        P("filter", "dp", None),
        P(None, "filter", None),
        P(None, "filter", None),
        P("dp"),
    )
    return jax.shard_map(
        shards,
        mesh=mesh,
        in_specs=placed,
        out_specs=(
            P("filter", "dp", None),
            P("filter", "dp", None),
            P(None, "filter", None),
            P(None, "filter", None),
        ),
        check_vma=False,
    )
```

```python
import functools

import jax
import jax.numpy as jnp
from jax import lax
from jax.experimental import pallas as pl
from jax.experimental.pallas import tpu as pltpu
from jax.sharding import PartitionSpec as P

PX = 8
PY = 16
PZ = 16
CAP = 3
CELLS = 2048
PLANE = PY * PZ
C = 256
BLK = 16
TAPS = 27
ROWS = TAPS * BLK

SIDE = 4


def axis_masks():
    cell = lax.broadcasted_iota(jnp.int32, (BLK, CELLS), 1)
    pos_y = (cell >> 4) & 15
    pos_z = cell & 15
    in_y = {-1: pos_y > 0, 0: None, 1: pos_y < PY - 1}
    in_z = {-1: pos_z > 0, 0: None, 1: pos_z < PZ - 1}
    return in_y, in_z


def shift_x(v, ox):
    if ox == 0:
        return v
    zero = jnp.zeros((v.shape[0], PLANE), v.dtype)
    if ox > 0:
        return jnp.concatenate([v[:, PLANE:], zero], axis=1)
    return jnp.concatenate([zero, v[:, :-PLANE]], axis=1)


def shift_yz(v, oy, oz, masks):
    step = oy * PZ + oz
    if step == 0:
        return v
    v = pltpu.roll(v, (-step) % CELLS, 1)
    for inside in (masks[0][oy], masks[1][oz]):
        if inside is not None:
            v = jnp.where(inside, v, 0.0)
    return v


def tap_conv(w_ref, full, sign, masks):
    proj = [
        jnp.dot(w_ref[k * 9 * BLK:(k + 1) * 9 * BLK, :], full, preferred_element_type=jnp.float32)
        for k in range(3)
    ]
    total = None
    for oy in (-1, 0, 1):
        for oz in (-1, 0, 1):
            at = (3 * (oy + 1) + oz + 1) * BLK
            part = None
            for ox in (-1, 0, 1):
                term = shift_x(proj[ox + 1][at:at + BLK, :], sign * ox)
                part = term if part is None else part + term
            part = shift_yz(part, sign * oy, sign * oz, masks)
            total = part if total is None else total + part
    return total


def tap_stack(stack_ref, v, sign, masks):
    for oy in (-1, 0, 1):
        for oz in (-1, 0, 1):
            moved = shift_yz(v, sign * oy, sign * oz, masks)
            for ox in (-1, 0, 1):
                t = 9 * (ox + 1) + 3 * (oy + 1) + (oz + 1)
                stack_ref[t * BLK:(t + 1) * BLK, :] = shift_x(moved, sign * ox).astype(jnp.bfloat16)


def place(scalars, pieces, full_ref, outer_is_x):
    x, y, sign = scalars[1], scalars[2], scalars[3]
    for outer in range(SIDE):
        for inner in range(SIDE):
            if outer_is_x:
                bx, by = x + SIDE + sign * outer, y + inner
            else:
                bx, by = x + inner, y + SIDE + sign * outer
            block = lax.rem(bx, SIDE) * SIDE + lax.rem(by, SIDE)
            at = pl.multiple_of(block * BLK, BLK)
            full_ref[pl.ds(at, BLK), :] = pieces[outer][inner, 0]


def over_cells(a, b):
    return lax.dot_general(a, b, (((1,), (1,)), ((), ())), preferred_element_type=jnp.float32)


def kernel_one(scalars, *refs):
    px, gx = refs[0:4], refs[4:8]
    w1, w2t, hid_out, del_out, keep_out, send_out, full_p, full_g, stack, grads = refs[8:]
    s = pl.program_id(0)
    core = scalars[4]

    @pl.when(s == 0)
    def _():
        grads[...] = jnp.zeros_like(grads)

    @pl.when(s >= scalars[0])
    def _():
        hid_out[...] = jnp.zeros_like(hid_out)
        del_out[...] = jnp.zeros_like(del_out)

    @pl.when(s < scalars[0])
    def _():
        masks = axis_masks()
        place(scalars, px, full_p, True)
        place(scalars, gx, full_g, False)
        first = tap_conv(w1, full_p[...], 1, masks)
        hidden_grad = tap_conv(w2t, full_g[...], -1, masks)
        sigma = 1.0 / (1.0 + jnp.exp(-first))
        hidden = (first * sigma).astype(jnp.bfloat16)
        delta = (hidden_grad * sigma * (1.0 + first * (1.0 - sigma))).astype(jnp.bfloat16)
        hid_out[0] = hidden
        del_out[0] = delta
        tap_stack(stack, delta.astype(jnp.float32), -1, masks)
        grads[0] += over_cells(full_p[...], stack[...])
        tap_stack(stack, hidden.astype(jnp.float32), 1, masks)
        grads[1] += over_cells(full_g[...], stack[...])

    @pl.when(s == pl.num_programs(0) - 1)
    def _():
        keep_out[...] = grads[core]
        send_out[...] = grads[1 - core]


def kernel_two(scalars, *refs):
    hx, dx = refs[0:4], refs[4:8]
    w2, w1t, out_ref, in_ref, full_h, full_d = refs[8:]
    s = pl.program_id(0)

    @pl.when(s >= scalars[0])
    def _():
        out_ref[...] = jnp.zeros_like(out_ref)
        in_ref[...] = jnp.zeros_like(in_ref)

    @pl.when(s < scalars[0])
    def _():
        masks = axis_masks()
        place(scalars, hx, full_h, True)
        place(scalars, dx, full_d, False)
        out_ref[0] = tap_conv(w2, full_h[...], 1, masks)
        in_ref[0] = tap_conv(w1t, full_d[...], -1, masks)


def from_near(axis, step):
    def at(x, y):
        return (x % SIDE) * SIDE + y % SIDE

    sides = [(x, y) for x in range(SIDE) for y in range(SIDE)]
    if axis == "x":
        return [(at(x + step, y), at(x, y)) for x, y in sides]
    return [(at(x, y + step), at(x, y)) for x, y in sides]


def from_mirrored(axis, step):
    pairs = []
    for d in range(BLK):
        for src, dst in from_near(axis, step if d % 2 == 0 else -step):
            pairs.append((d * BLK + src, d * BLK + dst))
    return pairs


def gather(v, inner, outer):
    near = [v] + [lax.ppermute(v, "filter", from_near(inner, k)) for k in (1, 2, 3)]
    own = jnp.stack(near)
    both = ("dp", "filter")
    ahead = lax.ppermute(own, both, from_mirrored(outer, 1))
    behind = lax.ppermute(own, both, from_mirrored(outer, 3))
    across = lax.ppermute(ahead, both, from_mirrored(outer, 1))
    return [own, ahead, across, behind]


def specs_of(count):
    piece = pl.BlockSpec((SIDE, 1, BLK, CELLS), lambda s, *_: (0, s, 0, 0))
    weight = pl.BlockSpec((ROWS, C), lambda s, *_: (0, 0))
    return [piece] * count + [weight] * 2


def slot_spec():
    return pl.BlockSpec((1, BLK, CELLS), lambda s, *_: (s, 0, 0))


def call_one(scalars, pieces, w1, w2t):
    slots = pieces[0].shape[1]
    flat = jax.ShapeDtypeStruct((slots, BLK, CELLS), jnp.bfloat16)
    return pl.pallas_call(
        kernel_one,
        name="layer_one",
        grid_spec=pltpu.PrefetchScalarGridSpec(
            num_scalar_prefetch=1,
            grid=(slots,),
            in_specs=specs_of(8),
            out_specs=[
                slot_spec(),
                slot_spec(),
                pl.BlockSpec((C, ROWS), lambda s, *_: (0, 0)),
                pl.BlockSpec((C, ROWS), lambda s, *_: (0, 0)),
            ],
            scratch_shapes=[
                pltpu.VMEM((C, CELLS), jnp.bfloat16),
                pltpu.VMEM((C, CELLS), jnp.bfloat16),
                pltpu.VMEM((ROWS, CELLS), jnp.bfloat16),
                pltpu.VMEM((2, C, ROWS), jnp.float32),
            ],
        ),
        out_shape=[flat, flat] + [jax.ShapeDtypeStruct((C, ROWS), jnp.float32)] * 2,
        compiler_params=pltpu.CompilerParams(vmem_limit_bytes=48 * 1024 * 1024),
        cost_estimate=pl.CostEstimate(
            flops=slots * 8 * ROWS * C * CELLS, transcendentals=slots * BLK * CELLS, bytes_accessed=slots * 4 * C * CELLS
        ),
    )(scalars, *pieces, w1, w2t)


def call_two(scalars, pieces, w2, w1t):
    slots = pieces[0].shape[1]
    flat = jax.ShapeDtypeStruct((slots, BLK, CELLS), jnp.float32)
    return pl.pallas_call(
        kernel_two,
        name="layer_two",
        grid_spec=pltpu.PrefetchScalarGridSpec(
            num_scalar_prefetch=1,
            grid=(slots,),
            in_specs=specs_of(8),
            out_specs=[slot_spec(), slot_spec()],
            scratch_shapes=[
                pltpu.VMEM((C, CELLS), jnp.bfloat16),
                pltpu.VMEM((C, CELLS), jnp.bfloat16),
            ],
        ),
        out_shape=[flat, flat],
        compiler_params=pltpu.CompilerParams(vmem_limit_bytes=48 * 1024 * 1024),
        cost_estimate=pl.CostEstimate(
            flops=slots * 4 * ROWS * C * CELLS, transcendentals=0, bytes_accessed=slots * 4 * C * CELLS
        ),
    )(scalars, *pieces, w2, w1t)


def kernel_split(w1, w2, out_ref):
    lane = lax.broadcasted_iota(jnp.int32, (BLK, 128), 1) >> 4
    for k, w in enumerate((w1, w2)):
        for half in range(2):
            for low in range(0, TAPS, 8):
                taps = range(low, min(low + 8, TAPS))
                tiles = [w[t, :, half * 128:(half + 1) * 128].astype(jnp.float32) for t in taps]
                for a in range(8):
                    total = None
                    for j, tile in enumerate(tiles):
                        amount = (BLK * (j - a)) % 128
                        moved = pltpu.roll(tile, amount, 1) if amount else tile
                        total = moved if total is None else jnp.where(lane == j, moved, total)
                    width = BLK * len(tiles)
                    out_ref[half * 8 + a, k, :, low * BLK:low * BLK + width] = total[:, :width].astype(jnp.bfloat16)


def split_weights(w1, w2):
    return pl.pallas_call(
        kernel_split,
        name="split_weights",
        out_shape=jax.ShapeDtypeStruct((BLK, 2, BLK, ROWS), jnp.bfloat16),
        cost_estimate=pl.CostEstimate(flops=0, transcendentals=0, bytes_accessed=4 * ROWS * C * 2),
    )(w1, w2)


def kernel_finish(scalars, own, other, first_ref, second_ref):
    @pl.when(scalars[4] == 0)
    def _():
        first_ref[...] = own[...].T
        second_ref[...] = other[...].T

    @pl.when(scalars[4] == 1)
    def _():
        first_ref[...] = other[...].T
        second_ref[...] = own[...].T


def finish(scalars, own, other):
    whole = pl.BlockSpec((C, ROWS), lambda i, *_: (0, 0))
    turned = pl.BlockSpec((ROWS, C), lambda i, *_: (0, 0))
    return pl.pallas_call(
        kernel_finish,
        name="finish_gradients",
        grid_spec=pltpu.PrefetchScalarGridSpec(
            num_scalar_prefetch=1, grid=(1,), in_specs=[whole, whole], out_specs=[turned, turned]
        ),
        out_shape=[jax.ShapeDtypeStruct((ROWS, C), jnp.float32)] * 2,
        cost_estimate=pl.CostEstimate(flops=0, transcendentals=0, bytes_accessed=16 * ROWS * C),
    )(scalars, own, other)


def sum_over_dp(scalars, keep, send):
    swap_cores = [(d, d ^ 1) for d in range(BLK)]
    by_core = [[2 * z + core for z in range(8)] for core in range(2)]
    total = keep + lax.ppermute(send, "dp", swap_cores)
    parts = lax.all_to_all(total.reshape(8, 32, ROWS), "dp", 0, 0, axis_index_groups=by_core, tiled=True)
    scale = 1.0 / jnp.sqrt(jnp.float32(lax.axis_size("dp") * CELLS))
    mine = parts.sum(axis=0) * scale

    odd = lax.axis_index("filter") % 2 == 1
    low, high = mine[:BLK], mine[BLK:]
    got = []
    for m in range(2):
        pairs = []
        for z in range(8):
            for f in range(BLK):
                j = (f + m) % 2
                pairs.append(((2 * z + 1) * BLK + f, (2 * (f // 2) + 1) * BLK + 2 * z + j))
        message = jnp.where(odd, low, high) if m else jnp.where(odd, high, low)
        got.append(lax.ppermute(message, ("dp", "filter"), pairs))
    halves = jnp.stack([jnp.where(odd, got[1], got[0]), jnp.where(odd, got[0], got[1])])
    second = halves.reshape(2, BLK, TAPS, BLK).transpose(0, 3, 2, 1).reshape(2 * BLK, ROWS)
    piece = jnp.where(scalars[4] == 0, mine, second)

    copies = jnp.broadcast_to(piece[None], (8, 2 * BLK, ROWS))
    own = lax.all_to_all(copies, "dp", 0, 0, axis_index_groups=by_core, tiled=True).reshape(C, ROWS)
    other = lax.ppermute(own, "dp", swap_cores)
    first_grad, second_grad = finish(scalars, own, other)
    return first_grad.reshape(TAPS, BLK, C), second_grad.reshape(TAPS, BLK, C)


def shards(patches, cotangent, first_weight, second_weight, counts):
    me = lax.axis_index("filter")
    core = lax.axis_index("dp") % 2
    scalars = jnp.stack([counts[0], me // SIDE, me % SIDE, 1 - 2 * core, core]).astype(jnp.int32)
    all_p = gather(patches.transpose(1, 0, 2), "y", "x")
    all_g = gather(cotangent.transpose(1, 0, 2), "x", "y")

    turned = lax.all_to_all(split_weights(first_weight, second_weight), "filter", 0, 0, tiled=True)
    w1t = turned[:, 0].reshape(C, ROWS).T
    w2t = turned[:, 1].reshape(C, ROWS).T
    w1 = first_weight.reshape(ROWS, C)
    w2 = second_weight.reshape(ROWS, C)

    hidden, delta, keep, send = call_one(scalars, all_p + all_g, w1, w2t)
    first_grad, second_grad = sum_over_dp(scalars, keep, send)

    all_h = gather(hidden, "y", "x")
    all_d = gather(delta, "x", "y")
    out, in_grad = call_two(scalars, all_h + all_d, w2, w1t)
    return (out.transpose(1, 0, 2), in_grad.transpose(1, 0, 2), first_grad, second_grad)


def solution(mesh):
    placed = (
        P("filter", "dp", None),
        P("filter", "dp", None),
        P(None, "filter", None),
        P(None, "filter", None),
        P("dp"),
    )
    return jax.shard_map(
        shards,
        mesh=mesh,
        in_specs=placed,
        out_specs=(
            P("filter", "dp", None),
            P("filter", "dp", None),
            P(None, "filter", None),
            P(None, "filter", None),
        ),
        check_vma=False,
    )
```

```python
import functools

import jax
import jax.numpy as jnp
from jax import lax
from jax.experimental import pallas as pl
from jax.experimental.pallas import tpu as pltpu
from jax.sharding import PartitionSpec as P

PX = 8
PY = 16
PZ = 16
CAP = 3
CELLS = 2048
PLANE = PY * PZ
C = 256
BLK = 16
TAPS = 27
ROWS = TAPS * BLK

SIDE = 4


def axis_masks():
    cell = lax.broadcasted_iota(jnp.int32, (BLK, CELLS), 1)
    pos_y = (cell >> 4) & 15
    pos_z = cell & 15
    in_y = {-1: pos_y > 0, 0: None, 1: pos_y < PY - 1}
    in_z = {-1: pos_z > 0, 0: None, 1: pos_z < PZ - 1}
    return in_y, in_z


def shift_x(v, ox):
    if ox == 0:
        return v
    zero = jnp.zeros((v.shape[0], PLANE), v.dtype)
    if ox > 0:
        return jnp.concatenate([v[:, PLANE:], zero], axis=1)
    return jnp.concatenate([zero, v[:, :-PLANE]], axis=1)


def shift_yz(v, oy, oz, masks):
    step = oy * PZ + oz
    if step == 0:
        return v
    v = pltpu.roll(v, (-step) % CELLS, 1)
    for inside in (masks[0][oy], masks[1][oz]):
        if inside is not None:
            v = jnp.where(inside, v, 0.0)
    return v


def tap_conv(w_ref, full, sign, masks):
    proj = [
        jnp.dot(w_ref[k * 9 * BLK:(k + 1) * 9 * BLK, :], full, preferred_element_type=jnp.float32)
        for k in range(3)
    ]
    total = None
    for oy in (-1, 0, 1):
        for oz in (-1, 0, 1):
            at = (3 * (oy + 1) + oz + 1) * BLK
            part = None
            for ox in (-1, 0, 1):
                term = shift_x(proj[ox + 1][at:at + BLK, :], sign * ox)
                part = term if part is None else part + term
            part = shift_yz(part, sign * oy, sign * oz, masks)
            total = part if total is None else total + part
    return total


def tap_stack(stack_ref, v, sign, masks):
    for oy in (-1, 0, 1):
        for oz in (-1, 0, 1):
            moved = shift_yz(v, sign * oy, sign * oz, masks)
            for ox in (-1, 0, 1):
                t = 9 * (ox + 1) + 3 * (oy + 1) + (oz + 1)
                stack_ref[t * BLK:(t + 1) * BLK, :] = shift_x(moved, sign * ox).astype(jnp.bfloat16)


def place(scalars, pieces, full_ref, outer_is_x):
    x, y, sign = scalars[1], scalars[2], scalars[3]
    for outer in range(SIDE):
        for inner in range(SIDE):
            if outer_is_x:
                bx, by = x + SIDE + sign * outer, y + inner
            else:
                bx, by = x + inner, y + SIDE + sign * outer
            block = lax.rem(bx, SIDE) * SIDE + lax.rem(by, SIDE)
            at = pl.multiple_of(block * BLK, BLK)
            full_ref[pl.ds(at, BLK), :] = pieces[outer][inner, 0]


def over_cells(a, b):
    return lax.dot_general(a, b, (((1,), (1,)), ((), ())), preferred_element_type=jnp.float32)


def kernel_one(scalars, *refs):
    px, gx = refs[0:4], refs[4:8]
    w1, w2t, hid_out, del_out, full_p, full_g = refs[8:]
    s = pl.program_id(0)

    @pl.when(s >= scalars[0])
    def _():
        hid_out[...] = jnp.zeros_like(hid_out)
        del_out[...] = jnp.zeros_like(del_out)

    @pl.when(s < scalars[0])
    def _():
        masks = axis_masks()
        place(scalars, px, full_p, True)
        place(scalars, gx, full_g, False)
        first = tap_conv(w1, full_p[...], 1, masks)
        hidden_grad = tap_conv(w2t, full_g[...], -1, masks)
        sigma = 1.0 / (1.0 + jnp.exp(-first))
        hid_out[0] = (first * sigma).astype(jnp.bfloat16)
        del_out[0] = (hidden_grad * sigma * (1.0 + first * (1.0 - sigma))).astype(jnp.bfloat16)


def kernel_grads(scalars, *refs):
    px, gx = refs[0:4], refs[4:8]
    hid, dlt, keep_out, send_out, full, stack, grads = refs[8:]
    s = pl.program_id(0)
    core = scalars[4]

    @pl.when(s == 0)
    def _():
        grads[...] = jnp.zeros_like(grads)

    @pl.when(s < scalars[0])
    def _():
        masks = axis_masks()
        place(scalars, px, full, True)
        tap_stack(stack, dlt[0].astype(jnp.float32), -1, masks)
        grads[0] += over_cells(full[...], stack[...])
        place(scalars, gx, full, False)
        tap_stack(stack, hid[0].astype(jnp.float32), 1, masks)
        grads[1] += over_cells(full[...], stack[...])

    @pl.when(s == pl.num_programs(0) - 1)
    def _():
        keep_out[...] = grads[core]
        send_out[...] = grads[1 - core]


def kernel_two(scalars, *refs):
    hx, dx = refs[0:4], refs[4:8]
    w2, w1t, out_ref, in_ref, full_h, full_d = refs[8:]
    s = pl.program_id(0)

    @pl.when(s >= scalars[0])
    def _():
        out_ref[...] = jnp.zeros_like(out_ref)
        in_ref[...] = jnp.zeros_like(in_ref)

    @pl.when(s < scalars[0])
    def _():
        masks = axis_masks()
        place(scalars, hx, full_h, True)
        place(scalars, dx, full_d, False)
        out_ref[0] = tap_conv(w2, full_h[...], 1, masks)
        in_ref[0] = tap_conv(w1t, full_d[...], -1, masks)


def from_near(axis, step):
    def at(x, y):
        return (x % SIDE) * SIDE + y % SIDE

    sides = [(x, y) for x in range(SIDE) for y in range(SIDE)]
    if axis == "x":
        return [(at(x + step, y), at(x, y)) for x, y in sides]
    return [(at(x, y + step), at(x, y)) for x, y in sides]


def from_mirrored(axis, step):
    pairs = []
    for d in range(BLK):
        for src, dst in from_near(axis, step if d % 2 == 0 else -step):
            pairs.append((d * BLK + src, d * BLK + dst))
    return pairs


def gather_near(v, inner, first=None):
    move = lambda k: lax.ppermute(v, "filter", from_near(inner, k))
    return jnp.stack([v, move(1) if first is None else first, move(2), move(3)])


def gather_far(own, outer):
    both = ("dp", "filter")
    return own, lax.ppermute(own, both, from_mirrored(outer, 1)), lax.ppermute(own, both, from_mirrored(outer, 3))


def gather_last(parts, outer):
    own, ahead, behind = parts
    return [own, ahead, lax.ppermute(ahead, ("dp", "filter"), from_mirrored(outer, 1)), behind]


def live_slot(s, scalars):
    return jnp.minimum(s, jnp.maximum(scalars[0] - 1, 0))


def piece_specs():
    return [pl.BlockSpec((SIDE, 1, BLK, CELLS), lambda s, sc: (0, live_slot(s, sc), 0, 0))] * 8


def weight_specs():
    return [pl.BlockSpec((ROWS, C), lambda s, *_: (0, 0))] * 2


def slot_spec():
    return pl.BlockSpec((1, BLK, CELLS), lambda s, *_: (s, 0, 0))


def params():
    return pltpu.CompilerParams(vmem_limit_bytes=48 * 1024 * 1024)


def call_one(scalars, pieces, w1, w2t):
    slots = pieces[0].shape[1]
    flat = jax.ShapeDtypeStruct((slots, BLK, CELLS), jnp.bfloat16)
    return pl.pallas_call(
        kernel_one,
        name="layer_one",
        grid_spec=pltpu.PrefetchScalarGridSpec(
            num_scalar_prefetch=1,
            grid=(slots,),
            in_specs=piece_specs() + weight_specs(),
            out_specs=[slot_spec(), slot_spec()],
            scratch_shapes=[pltpu.VMEM((C, CELLS), jnp.bfloat16)] * 2,
        ),
        out_shape=[flat, flat],
        compiler_params=params(),
        cost_estimate=pl.CostEstimate(
            flops=slots * 4 * ROWS * C * CELLS, transcendentals=slots * BLK * CELLS, bytes_accessed=slots * 4 * C * CELLS
        ),
    )(scalars, *pieces, w1, w2t)


def call_grads(scalars, pieces, hidden, delta):
    slots = pieces[0].shape[1]
    return pl.pallas_call(
        kernel_grads,
        name="weight_grads",
        grid_spec=pltpu.PrefetchScalarGridSpec(
            num_scalar_prefetch=1,
            grid=(slots,),
            in_specs=piece_specs() + [slot_spec(), slot_spec()],
            out_specs=[pl.BlockSpec((C, ROWS), lambda s, *_: (0, 0))] * 2,
            scratch_shapes=[
                pltpu.VMEM((C, CELLS), jnp.bfloat16),
                pltpu.VMEM((ROWS, CELLS), jnp.bfloat16),
                pltpu.VMEM((2, C, ROWS), jnp.float32),
            ],
        ),
        out_shape=[jax.ShapeDtypeStruct((C, ROWS), jnp.float32)] * 2,
        compiler_params=params(),
        cost_estimate=pl.CostEstimate(
            flops=slots * 4 * ROWS * C * CELLS, transcendentals=0, bytes_accessed=slots * 4 * C * CELLS
        ),
    )(scalars, *pieces, hidden, delta)


def call_two(scalars, pieces, w2, w1t):
    slots = pieces[0].shape[1]
    flat = jax.ShapeDtypeStruct((slots, BLK, CELLS), jnp.float32)
    return pl.pallas_call(
        kernel_two,
        name="layer_two",
        grid_spec=pltpu.PrefetchScalarGridSpec(
            num_scalar_prefetch=1,
            grid=(slots,),
            in_specs=piece_specs() + weight_specs(),
            out_specs=[slot_spec(), slot_spec()],
            scratch_shapes=[
                pltpu.VMEM((C, CELLS), jnp.bfloat16),
                pltpu.VMEM((C, CELLS), jnp.bfloat16),
            ],
        ),
        out_shape=[flat, flat],
        compiler_params=params(),
        cost_estimate=pl.CostEstimate(
            flops=slots * 160 * ROWS * C * CELLS, transcendentals=0, bytes_accessed=slots * 4 * C * CELLS
        ),
    )(scalars, *pieces, w2, w1t)


def kernel_split(w1, w2, out_ref):
    lane = lax.broadcasted_iota(jnp.int32, (BLK, 128), 1) >> 4
    for k, w in enumerate((w1, w2)):
        for half in range(2):
            for low in range(0, TAPS, 8):
                taps = range(low, min(low + 8, TAPS))
                tiles = [w[t, :, half * 128:(half + 1) * 128].astype(jnp.float32) for t in taps]
                for a in range(8):
                    total = None
                    for j, tile in enumerate(tiles):
                        amount = (BLK * (j - a)) % 128
                        moved = pltpu.roll(tile, amount, 1) if amount else tile
                        total = moved if total is None else jnp.where(lane == j, moved, total)
                    width = BLK * len(tiles)
                    out_ref[half * 8 + a, k, :, low * BLK:low * BLK + width] = total[:, :width].astype(jnp.bfloat16)


def split_weights(w1, w2):
    return pl.pallas_call(
        kernel_split,
        name="split_weights",
        out_shape=jax.ShapeDtypeStruct((BLK, 2, BLK, ROWS), jnp.bfloat16),
        cost_estimate=pl.CostEstimate(flops=0, transcendentals=0, bytes_accessed=4 * ROWS * C * 2),
    )(w1, w2)


def kernel_finish(scalars, own, other, first_ref, second_ref):
    @pl.when(scalars[4] == 0)
    def _():
        first_ref[...] = own[...].T
        second_ref[...] = other[...].T

    @pl.when(scalars[4] == 1)
    def _():
        first_ref[...] = other[...].T
        second_ref[...] = own[...].T


def finish(scalars, own, other):
    whole = pl.BlockSpec((C, ROWS), lambda i, *_: (0, 0))
    turned = pl.BlockSpec((ROWS, C), lambda i, *_: (0, 0))
    return pl.pallas_call(
        kernel_finish,
        name="finish_gradients",
        grid_spec=pltpu.PrefetchScalarGridSpec(
            num_scalar_prefetch=1, grid=(1,), in_specs=[whole, whole], out_specs=[turned, turned]
        ),
        out_shape=[jax.ShapeDtypeStruct((ROWS, C), jnp.float32)] * 2,
        cost_estimate=pl.CostEstimate(flops=0, transcendentals=0, bytes_accessed=16 * ROWS * C),
    )(scalars, own, other)


def sum_over_dp(scalars, keep, send):
    swap_cores = [(d, d ^ 1) for d in range(BLK)]
    by_core = [[2 * z + core for z in range(8)] for core in range(2)]
    total = keep + lax.ppermute(send, "dp", swap_cores)
    parts = lax.all_to_all(total.reshape(8, 32, ROWS), "dp", 0, 0, axis_index_groups=by_core, tiled=True)
    scale = 1.0 / jnp.sqrt(jnp.float32(lax.axis_size("dp") * CELLS))
    mine = parts.sum(axis=0) * scale

    odd = lax.axis_index("filter") % 2 == 1
    low, high = mine[:BLK], mine[BLK:]
    got = []
    for m in range(2):
        pairs = []
        for z in range(8):
            for f in range(BLK):
                j = (f + m) % 2
                pairs.append(((2 * z + 1) * BLK + f, (2 * (f // 2) + 1) * BLK + 2 * z + j))
        message = jnp.where(odd, low, high) if m else jnp.where(odd, high, low)
        got.append(lax.ppermute(message, ("dp", "filter"), pairs))
    halves = jnp.stack([jnp.where(odd, got[1], got[0]), jnp.where(odd, got[0], got[1])])
    second = halves.reshape(2, BLK, TAPS, BLK).transpose(0, 3, 2, 1).reshape(2 * BLK, ROWS)
    piece = jnp.where(scalars[4] == 0, mine, second)

    copies = jnp.broadcast_to(piece[None], (8, 2 * BLK, ROWS))
    own = lax.all_to_all(copies, "dp", 0, 0, axis_index_groups=by_core, tiled=True).reshape(C, ROWS)
    other = lax.ppermute(own, "dp", swap_cores)
    first_grad, second_grad = finish(scalars, own, other)
    return first_grad.reshape(TAPS, BLK, C), second_grad.reshape(TAPS, BLK, C)


def shards(patches, cotangent, first_weight, second_weight, counts):
    me = lax.axis_index("filter")
    core = lax.axis_index("dp") % 2
    scalars = jnp.stack([counts[0], me // SIDE, me % SIDE, 1 - 2 * core, core]).astype(jnp.int32)
    split = split_weights(first_weight, second_weight)
    near_p = gather_near(patches.transpose(1, 0, 2), "y")
    near_g = gather_near(cotangent.transpose(1, 0, 2), "x")
    near_g, split = lax.optimization_barrier((near_g, split))
    far_p = gather_far(near_p, "x")
    far_g = gather_far(near_g, "y")

    turned = lax.all_to_all(split, "filter", 0, 0, tiled=True)
    far_p, turned = lax.optimization_barrier((far_p, turned))
    all_p = gather_last(far_p, "x")
    all_g = gather_last(far_g, "y")
    w1t = turned[:, 0].reshape(C, ROWS).T
    w2t = turned[:, 1].reshape(C, ROWS).T
    w1 = first_weight.reshape(ROWS, C)
    w2 = second_weight.reshape(ROWS, C)

    hidden, delta = call_one(scalars, all_p + all_g, w1, w2t)
    first_h = lax.ppermute(hidden, "filter", from_near("y", 1))
    near_h = gather_near(hidden, "y", first_h)
    near_d = gather_near(delta, "x")
    keep, send = call_grads(scalars, all_p + all_g, hidden, delta)
    all_h = gather_last(gather_far(near_h, "x"), "x")
    all_d = gather_last(gather_far(near_d, "y"), "y")
    first_grad, second_grad = sum_over_dp(scalars, keep, send)
    out, in_grad = call_two(scalars, all_h + all_d, w2, w1t)
    return (out.transpose(1, 0, 2), in_grad.transpose(1, 0, 2), first_grad, second_grad)


def solution(mesh):
    placed = (
        P("filter", "dp", None),
        P("filter", "dp", None),
        P(None, "filter", None),
        P(None, "filter", None),
        P("dp"),
    )
    return jax.shard_map(
        shards,
        mesh=mesh,
        in_specs=placed,
        out_specs=(
            P("filter", "dp", None),
            P("filter", "dp", None),
            P(None, "filter", None),
            P(None, "filter", None),
        ),
        check_vma=False,
    )
```

```python
import functools

import jax
import jax.numpy as jnp
from jax import lax
from jax.experimental import pallas as pl
from jax.experimental.pallas import tpu as pltpu
from jax.sharding import PartitionSpec as P

PX = 8
PY = 16
PZ = 16
CAP = 3
CELLS = 2048
PLANE = PY * PZ
C = 256
BLK = 16
TAPS = 27
ROWS = TAPS * BLK

SIDE = 4


def axis_masks():
    cell = lax.broadcasted_iota(jnp.int32, (BLK, CELLS), 1)
    pos_y = (cell >> 4) & 15
    pos_z = cell & 15
    in_y = {-1: pos_y > 0, 0: None, 1: pos_y < PY - 1}
    in_z = {-1: pos_z > 0, 0: None, 1: pos_z < PZ - 1}
    return in_y, in_z


def shift_x(v, ox):
    if ox == 0:
        return v
    zero = jnp.zeros((v.shape[0], PLANE), v.dtype)
    if ox > 0:
        return jnp.concatenate([v[:, PLANE:], zero], axis=1)
    return jnp.concatenate([zero, v[:, :-PLANE]], axis=1)


def shift_yz(v, oy, oz, masks):
    step = oy * PZ + oz
    if step == 0:
        return v
    v = pltpu.roll(v, (-step) % CELLS, 1)
    for inside in (masks[0][oy], masks[1][oz]):
        if inside is not None:
            v = jnp.where(inside, v, 0.0)
    return v


def tap_conv(w_ref, full, sign, masks):
    proj = [
        jnp.dot(w_ref[k * 9 * BLK:(k + 1) * 9 * BLK, :], full, preferred_element_type=jnp.float32)
        for k in range(3)
    ]
    total = None
    for oy in (-1, 0, 1):
        for oz in (-1, 0, 1):
            at = (3 * (oy + 1) + oz + 1) * BLK
            part = None
            for ox in (-1, 0, 1):
                term = shift_x(proj[ox + 1][at:at + BLK, :], sign * ox)
                part = term if part is None else part + term
            part = shift_yz(part, sign * oy, sign * oz, masks)
            total = part if total is None else total + part
    return total


def tap_stack(stack_ref, v, sign, masks):
    for oy in (-1, 0, 1):
        for oz in (-1, 0, 1):
            moved = shift_yz(v, sign * oy, sign * oz, masks)
            for ox in (-1, 0, 1):
                t = 9 * (ox + 1) + 3 * (oy + 1) + (oz + 1)
                stack_ref[t * BLK:(t + 1) * BLK, :] = shift_x(moved, sign * ox).astype(jnp.bfloat16)


def place(scalars, pieces, full_ref, sign):
    x, y, core = scalars[1], scalars[2], scalars[3]
    for outer in range(SIDE):
        for inner in range(SIDE):
            far, near = SIDE + sign * outer, SIDE + inner
            bx = x + jnp.where(core == 0, far, near)
            by = y + jnp.where(core == 0, near, far)
            block = lax.rem(bx, SIDE) * SIDE + lax.rem(by, SIDE)
            at = pl.multiple_of(block * BLK, BLK)
            full_ref[pl.ds(at, BLK), :] = pieces[outer][inner, 0]


def over_cells(a, b):
    return lax.dot_general(a, b, (((1,), (1,)), ((), ())), preferred_element_type=jnp.float32)


def kernel_one(scalars, *refs):
    px, gx = refs[0:4], refs[4:8]
    w1, w2t, pair_out, full_p, full_g = refs[8:]
    s = pl.program_id(0)

    @pl.when(s >= scalars[0])
    def _():
        pair_out[...] = jnp.zeros_like(pair_out)

    @pl.when(s < scalars[0])
    def _():
        masks = axis_masks()
        place(scalars, px, full_p, 1)
        place(scalars, gx, full_g, -1)
        first = tap_conv(w1, full_p[...], 1, masks)
        hidden_grad = tap_conv(w2t, full_g[...], -1, masks)
        sigma = 1.0 / (1.0 + jnp.exp(-first))
        pair_out[0, 0] = (first * sigma).astype(jnp.bfloat16)
        pair_out[1, 0] = (hidden_grad * sigma * (1.0 + first * (1.0 - sigma))).astype(jnp.bfloat16)


def kernel_grads(scalars, *refs):
    px, gx = refs[0:4], refs[4:8]
    pair, keep_out, send_out, full, stack, grads = refs[8:]
    s = pl.program_id(0)
    core = scalars[3]

    @pl.when(s == 0)
    def _():
        grads[...] = jnp.zeros_like(grads)

    @pl.when(s < scalars[0])
    def _():
        masks = axis_masks()
        place(scalars, px, full, 1)
        tap_stack(stack, pair[1, 0].astype(jnp.float32), -1, masks)
        grads[0] += over_cells(full[...], stack[...])
        place(scalars, gx, full, -1)
        tap_stack(stack, pair[0, 0].astype(jnp.float32), 1, masks)
        grads[1] += over_cells(full[...], stack[...])

    @pl.when(s == pl.num_programs(0) - 1)
    def _():
        keep_out[...] = grads[core]
        send_out[...] = grads[1 - core]


def kernel_two(scalars, *refs):
    hx, dx = refs[0:4], refs[4:8]
    w2, w1t, out_ref, in_ref, full_h, full_d = refs[8:]
    s = pl.program_id(0)

    @pl.when(s >= scalars[0])
    def _():
        out_ref[...] = jnp.zeros_like(out_ref)
        in_ref[...] = jnp.zeros_like(in_ref)

    @pl.when(s < scalars[0])
    def _():
        masks = axis_masks()
        place(scalars, hx, full_h, 1)
        place(scalars, dx, full_d, -1)
        out_ref[0] = tap_conv(w2, full_h[...], 1, masks)
        in_ref[0] = tap_conv(w1t, full_d[...], -1, masks)


def from_axis(axes, step):
    pairs = []
    for d in range(BLK):
        for x in range(SIDE):
            for y in range(SIDE):
                sx, sy = (x + step, y) if axes[d % 2] == "x" else (x, y + step)
                pairs.append((d * BLK + (sx % SIDE) * SIDE + sy % SIDE, d * BLK + x * SIDE + y))
    return pairs


def turn(v, axes, step):
    return lax.ppermute(v, ("dp", "filter"), from_axis(axes, step))


def gather_near(pair):
    near = [pair] + [turn(pair, "yx", k) for k in (1, 2, 3)]
    return [jnp.stack([v[k] for v in near]) for k in range(2)]


def gather_far(nears):
    return [(own, turn(own, "xy", sign), turn(own, "xy", -sign)) for own, sign in zip(nears, (1, -1))]


def gather_last(parts):
    pieces = []
    for (own, ahead, behind), sign in zip(parts, (1, -1)):
        pieces += [own, ahead, turn(ahead, "xy", sign), behind]
    return pieces


def live_slot(s, scalars):
    return jnp.minimum(s, jnp.maximum(scalars[0] - 1, 0))


def piece_specs():
    return [pl.BlockSpec((SIDE, 1, BLK, CELLS), lambda s, sc: (0, live_slot(s, sc), 0, 0))] * 8


def weight_specs():
    return [pl.BlockSpec((ROWS, C), lambda s, *_: (0, 0))] * 2


def slot_spec():
    return pl.BlockSpec((1, BLK, CELLS), lambda s, *_: (s, 0, 0))


def pair_spec():
    return pl.BlockSpec((2, 1, BLK, CELLS), lambda s, *_: (0, s, 0, 0))


def params():
    return pltpu.CompilerParams(vmem_limit_bytes=48 * 1024 * 1024)


def call_one(scalars, pieces, w1, w2t):
    slots = pieces[0].shape[1]
    pair = jax.ShapeDtypeStruct((2, slots, BLK, CELLS), jnp.bfloat16)
    return pl.pallas_call(
        kernel_one,
        name="layer_one",
        grid_spec=pltpu.PrefetchScalarGridSpec(
            num_scalar_prefetch=1,
            grid=(slots,),
            in_specs=piece_specs() + weight_specs(),
            out_specs=pair_spec(),
            scratch_shapes=[pltpu.VMEM((C, CELLS), jnp.bfloat16)] * 2,
        ),
        out_shape=pair,
        compiler_params=params(),
        cost_estimate=pl.CostEstimate(
            flops=slots * 4 * ROWS * C * CELLS, transcendentals=slots * BLK * CELLS, bytes_accessed=slots * 4 * C * CELLS
        ),
    )(scalars, *pieces, w1, w2t)


def call_grads(scalars, pieces, pair):
    slots = pieces[0].shape[1]
    return pl.pallas_call(
        kernel_grads,
        name="weight_grads",
        grid_spec=pltpu.PrefetchScalarGridSpec(
            num_scalar_prefetch=1,
            grid=(slots,),
            in_specs=piece_specs() + [pair_spec()],
            out_specs=[pl.BlockSpec((C, ROWS), lambda s, *_: (0, 0))] * 2,
            scratch_shapes=[
                pltpu.VMEM((C, CELLS), jnp.bfloat16),
                pltpu.VMEM((ROWS, CELLS), jnp.bfloat16),
                pltpu.VMEM((2, C, ROWS), jnp.float32),
            ],
        ),
        out_shape=[jax.ShapeDtypeStruct((C, ROWS), jnp.float32)] * 2,
        compiler_params=params(),
        cost_estimate=pl.CostEstimate(
            flops=slots * 4 * ROWS * C * CELLS, transcendentals=0, bytes_accessed=slots * 4 * C * CELLS
        ),
    )(scalars, *pieces, pair)


def call_two(scalars, pieces, w2, w1t):
    slots = pieces[0].shape[1]
    flat = jax.ShapeDtypeStruct((slots, BLK, CELLS), jnp.float32)
    return pl.pallas_call(
        kernel_two,
        name="layer_two",
        grid_spec=pltpu.PrefetchScalarGridSpec(
            num_scalar_prefetch=1,
            grid=(slots,),
            in_specs=piece_specs() + weight_specs(),
            out_specs=[slot_spec(), slot_spec()],
            scratch_shapes=[
                pltpu.VMEM((C, CELLS), jnp.bfloat16),
                pltpu.VMEM((C, CELLS), jnp.bfloat16),
            ],
        ),
        out_shape=[flat, flat],
        compiler_params=params(),
        cost_estimate=pl.CostEstimate(
            flops=slots * 160 * ROWS * C * CELLS, transcendentals=0, bytes_accessed=slots * 4 * C * CELLS
        ),
    )(scalars, *pieces, w2, w1t)


def kernel_split(scalars, w1, w2, out_ref):
    lane = lax.broadcasted_iota(jnp.int32, (BLK, 128), 1) >> 4

    def split(w):
        for half in range(2):
            for low in range(0, TAPS, 8):
                taps = range(low, min(low + 8, TAPS))
                tiles = [w[t, :, half * 128:(half + 1) * 128].astype(jnp.float32) for t in taps]
                for a in range(8):
                    total = None
                    for j, tile in enumerate(tiles):
                        amount = (BLK * (j - a)) % 128
                        moved = pltpu.roll(tile, amount, 1) if amount else tile
                        total = moved if total is None else jnp.where(lane == j, moved, total)
                    width = BLK * len(tiles)
                    out_ref[half * 8 + a, :, low * BLK:low * BLK + width] = total[:, :width].astype(jnp.bfloat16)

    @pl.when(scalars[3] == 0)
    def _():
        split(w1)

    @pl.when(scalars[3] == 1)
    def _():
        split(w2)


def split_weights(scalars, w1, w2):
    whole = pl.BlockSpec((TAPS, BLK, C), lambda i, *_: (0, 0, 0))
    return pl.pallas_call(
        kernel_split,
        name="split_weights",
        grid_spec=pltpu.PrefetchScalarGridSpec(
            num_scalar_prefetch=1,
            grid=(1,),
            in_specs=[whole, whole],
            out_specs=pl.BlockSpec((BLK, BLK, ROWS), lambda i, *_: (0, 0, 0)),
        ),
        out_shape=jax.ShapeDtypeStruct((BLK, BLK, ROWS), jnp.bfloat16),
        cost_estimate=pl.CostEstimate(flops=0, transcendentals=0, bytes_accessed=4 * ROWS * C * 2),
    )(scalars, w1, w2)


def kernel_finish(scalars, own, other, first_ref, second_ref):
    @pl.when(scalars[3] == 0)
    def _():
        first_ref[...] = own[...].T
        second_ref[...] = other[...].T

    @pl.when(scalars[3] == 1)
    def _():
        first_ref[...] = other[...].T
        second_ref[...] = own[...].T


def finish(scalars, own, other):
    whole = pl.BlockSpec((C, ROWS), lambda i, *_: (0, 0))
    turned = pl.BlockSpec((ROWS, C), lambda i, *_: (0, 0))
    return pl.pallas_call(
        kernel_finish,
        name="finish_gradients",
        grid_spec=pltpu.PrefetchScalarGridSpec(
            num_scalar_prefetch=1, grid=(1,), in_specs=[whole, whole], out_specs=[turned, turned]
        ),
        out_shape=[jax.ShapeDtypeStruct((ROWS, C), jnp.float32)] * 2,
        cost_estimate=pl.CostEstimate(flops=0, transcendentals=0, bytes_accessed=16 * ROWS * C),
    )(scalars, own, other)


def swap_cores(v):
    return lax.ppermute(v, "dp", [(d, d ^ 1) for d in range(BLK)])


def sum_over_dp(scalars, keep, send):
    by_core = [[2 * z + core for z in range(8)] for core in range(2)]
    total = keep + swap_cores(send)
    parts = lax.all_to_all(total.reshape(8, 32, ROWS), "dp", 0, 0, axis_index_groups=by_core, tiled=True)
    scale = 1.0 / jnp.sqrt(jnp.float32(lax.axis_size("dp") * CELLS))
    mine = parts.sum(axis=0) * scale

    odd = lax.axis_index("filter") % 2 == 1
    low, high = mine[:BLK], mine[BLK:]
    got = []
    for m in range(2):
        pairs = []
        for z in range(8):
            for f in range(BLK):
                j = (f + m) % 2
                pairs.append(((2 * z + 1) * BLK + f, (2 * (f // 2) + 1) * BLK + 2 * z + j))
        message = jnp.where(odd, low, high) if m else jnp.where(odd, high, low)
        got.append(lax.ppermute(message, ("dp", "filter"), pairs))
    halves = jnp.stack([jnp.where(odd, got[1], got[0]), jnp.where(odd, got[0], got[1])])
    second = halves.reshape(2, BLK, TAPS, BLK).transpose(0, 3, 2, 1).reshape(2 * BLK, ROWS)
    piece = jnp.where(scalars[3] == 0, mine, second)

    copies = jnp.broadcast_to(piece[None], (8, 2 * BLK, ROWS))
    return lax.all_to_all(copies, "dp", 0, 0, axis_index_groups=by_core, tiled=True).reshape(C, ROWS)


def both_gradients(scalars, own):
    first_grad, second_grad = finish(scalars, own, swap_cores(own))
    return first_grad.reshape(TAPS, BLK, C), second_grad.reshape(TAPS, BLK, C)


def shards(patches, cotangent, first_weight, second_weight, counts):
    me = lax.axis_index("filter")
    core = lax.axis_index("dp") % 2
    scalars = jnp.stack([counts[0], me // SIDE, me % SIDE, core]).astype(jnp.int32)
    split = split_weights(scalars, first_weight, second_weight)
    nears = gather_near(jnp.stack([patches.transpose(1, 0, 2), cotangent.transpose(1, 0, 2)]))
    nears, split = lax.optimization_barrier((nears, split))
    fars = gather_far(nears)

    turned = lax.all_to_all(split, "filter", 0, 0, tiled=True).reshape(C, ROWS)
    fars, turned = lax.optimization_barrier((fars, turned))
    pieces = gather_last(fars)
    other = swap_cores(turned)
    w1t = jnp.where(core == 0, turned, other).T
    w2t = jnp.where(core == 0, other, turned).T
    w1 = first_weight.reshape(ROWS, C)
    w2 = second_weight.reshape(ROWS, C)

    pair = call_one(scalars, pieces, w1, w2t)
    second_pieces = gather_last(gather_far(gather_near(pair)))
    keep, send = call_grads(scalars, pieces, pair)
    own = sum_over_dp(scalars, keep, send)
    out, in_grad = call_two(scalars, second_pieces, w2, w1t)
    out, in_grad, own = lax.optimization_barrier((out, in_grad, own))
    first_grad, second_grad = both_gradients(scalars, own)
    return (out.transpose(1, 0, 2), in_grad.transpose(1, 0, 2), first_grad, second_grad)


def solution(mesh):
    placed = (
        P("filter", "dp", None),
        P("filter", "dp", None),
        P(None, "filter", None),
        P(None, "filter", None),
        P("dp"),
    )
    return jax.shard_map(
        shards,
        mesh=mesh,
        in_specs=placed,
        out_specs=(
            P("filter", "dp", None),
            P("filter", "dp", None),
            P(None, "filter", None),
            P(None, "filter", None),
        ),
        check_vma=False,
    )
```

```python
import functools

import jax
import jax.numpy as jnp
from jax import lax
from jax.experimental import pallas as pl
from jax.experimental.pallas import tpu as pltpu
from jax.sharding import PartitionSpec as P

PX = 8
PY = 16
PZ = 16
CAP = 3
CELLS = 2048
PLANE = PY * PZ
C = 256
BLK = 16
TAPS = 27
ROWS = TAPS * BLK

SIDE = 4
HALF = (8, 2, BLK, ROWS)


def axis_masks():
    cell = lax.broadcasted_iota(jnp.int32, (BLK, CELLS), 1)
    pos_y = (cell >> 4) & 15
    pos_z = cell & 15
    in_y = {-1: pos_y > 0, 0: None, 1: pos_y < PY - 1}
    in_z = {-1: pos_z > 0, 0: None, 1: pos_z < PZ - 1}
    return in_y, in_z


def shift_x(v, ox):
    if ox == 0:
        return v
    zero = jnp.zeros((v.shape[0], PLANE), v.dtype)
    if ox > 0:
        return jnp.concatenate([v[:, PLANE:], zero], axis=1)
    return jnp.concatenate([zero, v[:, :-PLANE]], axis=1)


def shift_yz(v, oy, oz, masks):
    step = oy * PZ + oz
    if step == 0:
        return v
    v = pltpu.roll(v, (-step) % CELLS, 1)
    for inside in (masks[0][oy], masks[1][oz]):
        if inside is not None:
            v = jnp.where(inside, v, 0.0)
    return v


def tap_conv(w_ref, full, sign, masks):
    proj = [
        jnp.dot(w_ref[k * 9 * BLK:(k + 1) * 9 * BLK, :], full, preferred_element_type=jnp.float32)
        for k in range(3)
    ]
    total = None
    for oy in (-1, 0, 1):
        for oz in (-1, 0, 1):
            at = (3 * (oy + 1) + oz + 1) * BLK
            part = None
            for ox in (-1, 0, 1):
                term = shift_x(proj[ox + 1][at:at + BLK, :], sign * ox)
                part = term if part is None else part + term
            part = shift_yz(part, sign * oy, sign * oz, masks)
            total = part if total is None else total + part
    return total


def tap_stack(stack_ref, v, sign, masks):
    for oy in (-1, 0, 1):
        for oz in (-1, 0, 1):
            moved = shift_yz(v, sign * oy, sign * oz, masks)
            for ox in (-1, 0, 1):
                t = 9 * (ox + 1) + 3 * (oy + 1) + (oz + 1)
                stack_ref[t * BLK:(t + 1) * BLK, :] = shift_x(moved, sign * ox).astype(jnp.bfloat16)


def place(scalars, pieces, full_ref, sign):
    x, y, core = scalars[1], scalars[2], scalars[3]
    for outer in range(SIDE):
        for inner in range(SIDE):
            far, near = SIDE + sign * outer, SIDE + inner
            bx = x + jnp.where(core == 0, far, near)
            by = y + jnp.where(core == 0, near, far)
            block = lax.rem(bx, SIDE) * SIDE + lax.rem(by, SIDE)
            at = pl.multiple_of(block * BLK, BLK)
            full_ref[pl.ds(at, BLK), :] = pieces[outer][inner, 0]


def over_cells(a, b):
    return lax.dot_general(a, b, (((1,), (1,)), ((), ())), preferred_element_type=jnp.float32)


def kernel_one(scalars, *refs):
    px, gx = refs[0:4], refs[4:8]
    w1, w2t, pair_out, full_p, full_g = refs[8:]
    s = pl.program_id(0)

    @pl.when(s >= scalars[0])
    def _():
        pair_out[...] = jnp.zeros_like(pair_out)

    @pl.when(s < scalars[0])
    def _():
        masks = axis_masks()
        place(scalars, px, full_p, 1)
        place(scalars, gx, full_g, -1)
        first = tap_conv(w1, full_p[...], 1, masks)
        hidden_grad = tap_conv(w2t, full_g[...], -1, masks)
        sigma = 1.0 / (1.0 + jnp.exp(-first))
        pair_out[0, 0] = (first * sigma).astype(jnp.bfloat16)
        pair_out[1, 0] = (hidden_grad * sigma * (1.0 + first * (1.0 - sigma))).astype(jnp.bfloat16)


def kernel_grads(scalars, *refs):
    px, gx = refs[0:4], refs[4:8]
    pair, keep_out, send_out, full, stack, grads = refs[8:]
    s = pl.program_id(0)
    core = scalars[3]

    @pl.when(s == 0)
    def _():
        grads[...] = jnp.zeros_like(grads)

    @pl.when(s < scalars[0])
    def _():
        masks = axis_masks()
        place(scalars, px, full, 1)
        tap_stack(stack, pair[1, 0].astype(jnp.float32), -1, masks)
        grads[0] += over_cells(full[...], stack[...])
        place(scalars, gx, full, -1)
        tap_stack(stack, pair[0, 0].astype(jnp.float32), 1, masks)
        grads[1] += over_cells(full[...], stack[...])

    @pl.when(s == pl.num_programs(0) - 1)
    def _():
        for z in range(8):
            for k in range(2):
                keep_out[z, k] = grads[k, pl.ds(pl.multiple_of((2 * z + core) * BLK, BLK), BLK), :]
                send_out[z, k] = grads[k, pl.ds(pl.multiple_of((2 * z + 1 - core) * BLK, BLK), BLK), :]


def kernel_two(scalars, *refs):
    hx, dx = refs[0:4], refs[4:8]
    w2, w1t, out_ref, in_ref, full_h, full_d = refs[8:]
    s = pl.program_id(0)

    @pl.when(s >= scalars[0])
    def _():
        out_ref[...] = jnp.zeros_like(out_ref)
        in_ref[...] = jnp.zeros_like(in_ref)

    @pl.when(s < scalars[0])
    def _():
        masks = axis_masks()
        place(scalars, hx, full_h, 1)
        place(scalars, dx, full_d, -1)
        out_ref[0] = tap_conv(w2, full_h[...], 1, masks)
        in_ref[0] = tap_conv(w1t, full_d[...], -1, masks)


def from_axis(axes, step):
    pairs = []
    for d in range(BLK):
        for x in range(SIDE):
            for y in range(SIDE):
                sx, sy = (x + step, y) if axes[d % 2] == "x" else (x, y + step)
                pairs.append((d * BLK + (sx % SIDE) * SIDE + sy % SIDE, d * BLK + x * SIDE + y))
    return pairs


def turn(v, axes, step):
    return lax.ppermute(v, ("dp", "filter"), from_axis(axes, step))


def gather_near(pair):
    near = [pair] + [turn(pair, "yx", k) for k in (1, 2, 3)]
    return [jnp.stack([v[k] for v in near]) for k in range(2)]


def gather_far(nears):
    return [(own, turn(own, "xy", sign), turn(own, "xy", -sign)) for own, sign in zip(nears, (1, -1))]


def gather_last(parts):
    pieces = []
    for (own, ahead, behind), sign in zip(parts, (1, -1)):
        pieces += [own, ahead, turn(ahead, "xy", sign), behind]
    return pieces


def live_slot(s, scalars):
    return jnp.minimum(s, jnp.maximum(scalars[0] - 1, 0))


def piece_specs():
    return [pl.BlockSpec((SIDE, 1, BLK, CELLS), lambda s, sc: (0, live_slot(s, sc), 0, 0))] * 8


def weight_specs():
    return [pl.BlockSpec((ROWS, C), lambda s, *_: (0, 0))] * 2


def slot_spec():
    return pl.BlockSpec((1, BLK, CELLS), lambda s, *_: (s, 0, 0))


def pair_spec():
    return pl.BlockSpec((2, 1, BLK, CELLS), lambda s, *_: (0, s, 0, 0))


def params():
    return pltpu.CompilerParams(vmem_limit_bytes=48 * 1024 * 1024)


def call_one(scalars, pieces, w1, w2t):
    slots = pieces[0].shape[1]
    pair = jax.ShapeDtypeStruct((2, slots, BLK, CELLS), jnp.bfloat16)
    return pl.pallas_call(
        kernel_one,
        name="layer_one",
        grid_spec=pltpu.PrefetchScalarGridSpec(
            num_scalar_prefetch=1,
            grid=(slots,),
            in_specs=piece_specs() + weight_specs(),
            out_specs=pair_spec(),
            scratch_shapes=[pltpu.VMEM((C, CELLS), jnp.bfloat16)] * 2,
        ),
        out_shape=pair,
        compiler_params=params(),
        cost_estimate=pl.CostEstimate(
            flops=slots * 4 * ROWS * C * CELLS, transcendentals=slots * BLK * CELLS, bytes_accessed=slots * 4 * C * CELLS
        ),
    )(scalars, *pieces, w1, w2t)


def call_grads(scalars, pieces, pair):
    slots = pieces[0].shape[1]
    return pl.pallas_call(
        kernel_grads,
        name="weight_grads",
        grid_spec=pltpu.PrefetchScalarGridSpec(
            num_scalar_prefetch=1,
            grid=(slots,),
            in_specs=piece_specs() + [pair_spec()],
            out_specs=[pl.BlockSpec(HALF, lambda s, *_: (0, 0, 0, 0))] * 2,
            scratch_shapes=[
                pltpu.VMEM((C, CELLS), jnp.bfloat16),
                pltpu.VMEM((ROWS, CELLS), jnp.bfloat16),
                pltpu.VMEM((2, C, ROWS), jnp.float32),
            ],
        ),
        out_shape=[jax.ShapeDtypeStruct(HALF, jnp.float32)] * 2,
        compiler_params=params(),
        cost_estimate=pl.CostEstimate(
            flops=slots * 4 * ROWS * C * CELLS, transcendentals=0, bytes_accessed=slots * 4 * C * CELLS
        ),
    )(scalars, *pieces, pair)


def call_two(scalars, pieces, w2, w1t):
    slots = pieces[0].shape[1]
    flat = jax.ShapeDtypeStruct((slots, BLK, CELLS), jnp.float32)
    return pl.pallas_call(
        kernel_two,
        name="layer_two",
        grid_spec=pltpu.PrefetchScalarGridSpec(
            num_scalar_prefetch=1,
            grid=(slots,),
            in_specs=piece_specs() + weight_specs(),
            out_specs=[slot_spec(), slot_spec()],
            scratch_shapes=[
                pltpu.VMEM((C, CELLS), jnp.bfloat16),
                pltpu.VMEM((C, CELLS), jnp.bfloat16),
            ],
        ),
        out_shape=[flat, flat],
        compiler_params=params(),
        cost_estimate=pl.CostEstimate(
            flops=slots * 4 * ROWS * C * CELLS, transcendentals=0, bytes_accessed=slots * 4 * C * CELLS
        ),
    )(scalars, *pieces, w2, w1t)


def kernel_split(scalars, w1, w2, out_ref):
    lane = lax.broadcasted_iota(jnp.int32, (BLK, 128), 1) >> 4

    def split(w):
        for half in range(2):
            for low in range(0, TAPS, 8):
                taps = range(low, min(low + 8, TAPS))
                tiles = [w[t, :, half * 128:(half + 1) * 128].astype(jnp.float32) for t in taps]
                for a in range(8):
                    total = None
                    for j, tile in enumerate(tiles):
                        amount = (BLK * (j - a)) % 128
                        moved = pltpu.roll(tile, amount, 1) if amount else tile
                        total = moved if total is None else jnp.where(lane == j, moved, total)
                    width = BLK * len(tiles)
                    out_ref[half * 8 + a, :, low * BLK:low * BLK + width] = total[:, :width].astype(jnp.bfloat16)

    @pl.when(scalars[3] == 0)
    def _():
        split(w1)

    @pl.when(scalars[3] == 1)
    def _():
        split(w2)


def split_weights(scalars, w1, w2):
    whole = pl.BlockSpec((TAPS, BLK, C), lambda i, *_: (0, 0, 0))
    return pl.pallas_call(
        kernel_split,
        name="split_weights",
        grid_spec=pltpu.PrefetchScalarGridSpec(
            num_scalar_prefetch=1,
            grid=(1,),
            in_specs=[whole, whole],
            out_specs=pl.BlockSpec((BLK, BLK, ROWS), lambda i, *_: (0, 0, 0)),
        ),
        out_shape=jax.ShapeDtypeStruct((BLK, BLK, ROWS), jnp.bfloat16),
        cost_estimate=pl.CostEstimate(flops=0, transcendentals=0, bytes_accessed=4 * ROWS * C * 2),
    )(scalars, w1, w2)


def kernel_collect(mine, got, out_ref):
    lane = lax.broadcasted_iota(jnp.int32, (BLK, 128), 1) >> 4
    flipped = got[...].T
    wide = jnp.concatenate([flipped, jnp.zeros((ROWS, 128 - BLK), jnp.float32)], axis=1)
    for z in range(8):
        out_ref[z, 0] = mine[...]
    for low in range(0, TAPS, 8):
        total = None
        count = min(8, TAPS - low)
        for j in range(count):
            tile = wide[(low + j) * BLK:(low + j + 1) * BLK, :]
            moved = pltpu.roll(tile, BLK * j, 1) if j else tile
            total = moved if total is None else jnp.where(lane == j, moved, total)
        width = BLK * count
        for z in range(8):
            out_ref[z, 1, :, low * BLK:low * BLK + width] = total[:, :width]


def collect(mine, got):
    return pl.pallas_call(
        kernel_collect,
        name="collect_rows",
        out_shape=jax.ShapeDtypeStruct(HALF, jnp.float32),
        cost_estimate=pl.CostEstimate(flops=0, transcendentals=0, bytes_accessed=4 * ROWS * C),
    )(mine, got)


def kernel_finish(scalars, own, other, first_ref, second_ref, full):
    core = scalars[3]
    scale = 1.0 / (BLK * CELLS) ** 0.5
    for k, out_ref in enumerate((first_ref, second_ref)):
        for z in range(8):
            full[pl.ds(pl.multiple_of((2 * z + core) * BLK, BLK), BLK), :] = own[z, k]
            full[pl.ds(pl.multiple_of((2 * z + 1 - core) * BLK, BLK), BLK), :] = other[z, k]
        out_ref[...] = full[...].T * scale


def finish(scalars, own, other):
    half = pl.BlockSpec(HALF, lambda i, *_: (0, 0, 0, 0))
    turned = pl.BlockSpec((ROWS, C), lambda i, *_: (0, 0))
    return pl.pallas_call(
        kernel_finish,
        name="finish_gradients",
        grid_spec=pltpu.PrefetchScalarGridSpec(
            num_scalar_prefetch=1,
            grid=(1,),
            in_specs=[half, half],
            out_specs=[turned, turned],
            scratch_shapes=[pltpu.VMEM((C, ROWS), jnp.float32)],
        ),
        out_shape=[jax.ShapeDtypeStruct((ROWS, C), jnp.float32)] * 2,
        cost_estimate=pl.CostEstimate(flops=0, transcendentals=0, bytes_accessed=16 * ROWS * C),
    )(scalars, own, other)


def swap_cores(v):
    return lax.ppermute(v, "dp", [(d, d ^ 1) for d in range(BLK)])


def over_z(v):
    by_core = [[2 * z + core for z in range(8)] for core in range(2)]
    return lax.all_to_all(v, "dp", 0, 0, axis_index_groups=by_core, tiled=True)


def sum_over_dp(keep, send):
    mine = over_z(keep + swap_cores(send)).sum(axis=0)
    flip = [(d * BLK + f, f * BLK + d) for d in range(BLK) for f in range(BLK)]
    got = lax.ppermute(mine[1], ("dp", "filter"), flip)
    return over_z(collect(mine[0], got))


def both_gradients(scalars, own):
    first_grad, second_grad = finish(scalars, own, swap_cores(own))
    return first_grad.reshape(TAPS, BLK, C), second_grad.reshape(TAPS, BLK, C)


def shards(patches, cotangent, first_weight, second_weight, counts):
    me = lax.axis_index("filter")
    core = lax.axis_index("dp") % 2
    scalars = jnp.stack([counts[0], me // SIDE, me % SIDE, core]).astype(jnp.int32)
    split = split_weights(scalars, first_weight, second_weight)
    nears = gather_near(jnp.stack([patches.transpose(1, 0, 2), cotangent.transpose(1, 0, 2)]))
    nears, split = lax.optimization_barrier((nears, split))
    fars = gather_far(nears)

    turned = lax.all_to_all(split, "filter", 0, 0, tiled=True).reshape(C, ROWS)
    pieces = gather_last(fars)
    other = swap_cores(turned)
    w1t = jnp.where(core == 0, turned, other).T
    w2t = jnp.where(core == 0, other, turned).T
    w1 = first_weight.reshape(ROWS, C)
    w2 = second_weight.reshape(ROWS, C)

    pair = call_one(scalars, pieces, w1, w2t)
    second_pieces = gather_last(gather_far(gather_near(pair)))
    keep, send = call_grads(scalars, pieces, pair)
    own = sum_over_dp(keep, send)
    out, in_grad = call_two(scalars, second_pieces, w2, w1t)
    out, in_grad, own = lax.optimization_barrier((out, in_grad, own))
    first_grad, second_grad = both_gradients(scalars, own)
    return (out.transpose(1, 0, 2), in_grad.transpose(1, 0, 2), first_grad, second_grad)


def solution(mesh):
    placed = (
        P("filter", "dp", None),
        P("filter", "dp", None),
        P(None, "filter", None),
        P(None, "filter", None),
        P("dp"),
    )
    return jax.shard_map(
        shards,
        mesh=mesh,
        in_specs=placed,
        out_specs=(
            P("filter", "dp", None),
            P("filter", "dp", None),
            P(None, "filter", None),
            P(None, "filter", None),
        ),
        check_vma=False,
    )
```

```python
import functools

import jax
import jax.numpy as jnp
from jax import lax
from jax.experimental import pallas as pl
from jax.experimental.pallas import tpu as pltpu
from jax.sharding import PartitionSpec as P

PX = 8
PY = 16
PZ = 16
CAP = 3
CELLS = 2048
PLANE = PY * PZ
C = 256
BLK = 16
TAPS = 27
ROWS = TAPS * BLK

SIDE = 4
HALF = (8, 2, BLK, ROWS)


def axis_masks():
    cell = lax.broadcasted_iota(jnp.int32, (BLK, CELLS), 1)
    pos_y = (cell >> 4) & 15
    pos_z = cell & 15
    in_y = {-1: pos_y > 0, 0: None, 1: pos_y < PY - 1}
    in_z = {-1: pos_z > 0, 0: None, 1: pos_z < PZ - 1}
    return in_y, in_z


def shift_x(v, ox):
    if ox == 0:
        return v
    zero = jnp.zeros((v.shape[0], PLANE), v.dtype)
    if ox > 0:
        return jnp.concatenate([v[:, PLANE:], zero], axis=1)
    return jnp.concatenate([zero, v[:, :-PLANE]], axis=1)


def shift_yz(v, oy, oz, masks):
    step = oy * PZ + oz
    if step == 0:
        return v
    v = pltpu.roll(v, (-step) % CELLS, 1)
    for inside in (masks[0][oy], masks[1][oz]):
        if inside is not None:
            v = jnp.where(inside, v, 0.0)
    return v


def tap_conv(w_ref, full, sign, masks):
    proj = [
        jnp.dot(w_ref[k * 9 * BLK:(k + 1) * 9 * BLK, :], full, preferred_element_type=jnp.float32)
        for k in range(3)
    ]
    total = None
    for oy in (-1, 0, 1):
        for oz in (-1, 0, 1):
            at = (3 * (oy + 1) + oz + 1) * BLK
            part = None
            for ox in (-1, 0, 1):
                term = shift_x(proj[ox + 1][at:at + BLK, :], sign * ox)
                part = term if part is None else part + term
            part = shift_yz(part, sign * oy, sign * oz, masks)
            total = part if total is None else total + part
    return total


def tap_stack(stack_ref, v, sign, masks):
    for oy in (-1, 0, 1):
        for oz in (-1, 0, 1):
            moved = shift_yz(v, sign * oy, sign * oz, masks)
            for ox in (-1, 0, 1):
                t = 9 * (ox + 1) + 3 * (oy + 1) + (oz + 1)
                stack_ref[t * BLK:(t + 1) * BLK, :] = shift_x(moved, sign * ox).astype(jnp.bfloat16)


def place(scalars, pieces, full_ref, sign):
    x, y, core = scalars[1], scalars[2], scalars[3]
    for outer in range(SIDE):
        for inner in range(SIDE):
            far, near = SIDE + sign * outer, SIDE + inner
            bx = x + jnp.where(core == 0, far, near)
            by = y + jnp.where(core == 0, near, far)
            block = lax.rem(bx, SIDE) * SIDE + lax.rem(by, SIDE)
            at = pl.multiple_of(block * BLK, BLK)
            full_ref[pl.ds(at, BLK), :] = pieces[outer][inner, 0]


def over_cells(a, b):
    return lax.dot_general(a, b, (((1,), (1,)), ((), ())), preferred_element_type=jnp.float32)


def kernel_one(scalars, *refs):
    px, gx = refs[0:4], refs[4:8]
    w1, w2t, pair_out, full_p, full_g = refs[8:]
    s = pl.program_id(0)

    @pl.when(s >= scalars[0])
    def _():
        pair_out[...] = jnp.zeros_like(pair_out)

    @pl.when(s < scalars[0])
    def _():
        masks = axis_masks()
        place(scalars, px, full_p, 1)
        place(scalars, gx, full_g, -1)
        first = tap_conv(w1, full_p[...], 1, masks)
        hidden_grad = tap_conv(w2t, full_g[...], -1, masks)
        sigma = 1.0 / (1.0 + jnp.exp(-first))
        pair_out[0, 0] = (first * sigma).astype(jnp.bfloat16)
        pair_out[1, 0] = (hidden_grad * sigma * (1.0 + first * (1.0 - sigma))).astype(jnp.bfloat16)


def kernel_grads(scalars, *refs):
    px, gx = refs[0:4], refs[4:8]
    pair, keep_out, send_out, full, stack, grads = refs[8:]
    s = pl.program_id(0)
    core = scalars[3]

    @pl.when(s == 0)
    def _():
        grads[...] = jnp.zeros_like(grads)

    @pl.when(s < scalars[0])
    def _():
        masks = axis_masks()
        place(scalars, px, full, 1)
        tap_stack(stack, pair[1, 0].astype(jnp.float32), -1, masks)
        grads[0] += over_cells(full[...], stack[...])
        place(scalars, gx, full, -1)
        tap_stack(stack, pair[0, 0].astype(jnp.float32), 1, masks)
        grads[1] += over_cells(full[...], stack[...])

    @pl.when(s == pl.num_programs(0) - 1)
    def _():
        for z in range(8):
            for k in range(2):
                keep_out[z, k] = grads[k, pl.ds(pl.multiple_of((2 * z + core) * BLK, BLK), BLK), :]
                send_out[z, k] = grads[k, pl.ds(pl.multiple_of((2 * z + 1 - core) * BLK, BLK), BLK), :]


def kernel_two(scalars, *refs):
    hx, dx = refs[0:4], refs[4:8]
    w2, w1t, out_ref, in_ref, full_h, full_d = refs[8:]
    s = pl.program_id(0)

    @pl.when(s >= scalars[0])
    def _():
        out_ref[...] = jnp.zeros_like(out_ref)
        in_ref[...] = jnp.zeros_like(in_ref)

    @pl.when(s < scalars[0])
    def _():
        masks = axis_masks()
        place(scalars, hx, full_h, 1)
        place(scalars, dx, full_d, -1)
        out_ref[0] = tap_conv(w2, full_h[...], 1, masks)
        in_ref[0] = tap_conv(w1t, full_d[...], -1, masks)


def from_axis(axes, step):
    pairs = []
    for d in range(BLK):
        for x in range(SIDE):
            for y in range(SIDE):
                sx, sy = (x + step, y) if axes[d % 2] == "x" else (x, y + step)
                pairs.append((d * BLK + (sx % SIDE) * SIDE + sy % SIDE, d * BLK + x * SIDE + y))
    return pairs


def turn(v, axes, step):
    return lax.ppermute(v, ("dp", "filter"), from_axis(axes, step))


def gather_near(pair):
    near = [pair] + [turn(pair, "yx", k) for k in (1, 2, 3)]
    return [jnp.stack([v[k] for v in near]) for k in range(2)]


def gather_far(nears):
    return [(own, turn(own, "xy", sign), turn(own, "xy", -sign)) for own, sign in zip(nears, (1, -1))]


def gather_last(parts):
    pieces = []
    for (own, ahead, behind), sign in zip(parts, (1, -1)):
        pieces += [own, ahead, turn(ahead, "xy", sign), behind]
    return pieces


def live_slot(s, scalars):
    return jnp.minimum(s, jnp.maximum(scalars[0] - 1, 0))


def piece_specs():
    return [pl.BlockSpec((SIDE, 1, BLK, CELLS), lambda s, sc: (0, live_slot(s, sc), 0, 0))] * 8


def weight_specs():
    return [pl.BlockSpec((ROWS, C), lambda s, *_: (0, 0))] * 2


def slot_spec():
    return pl.BlockSpec((1, BLK, CELLS), lambda s, *_: (s, 0, 0))


def pair_spec():
    return pl.BlockSpec((2, 1, BLK, CELLS), lambda s, *_: (0, s, 0, 0))


def params():
    return pltpu.CompilerParams(vmem_limit_bytes=48 * 1024 * 1024)


def call_one(scalars, pieces, w1, w2t):
    slots = pieces[0].shape[1]
    pair = jax.ShapeDtypeStruct((2, slots, BLK, CELLS), jnp.bfloat16)
    return pl.pallas_call(
        kernel_one,
        name="layer_one",
        grid_spec=pltpu.PrefetchScalarGridSpec(
            num_scalar_prefetch=1,
            grid=(slots,),
            in_specs=piece_specs() + weight_specs(),
            out_specs=pair_spec(),
            scratch_shapes=[pltpu.VMEM((C, CELLS), jnp.bfloat16)] * 2,
        ),
        out_shape=pair,
        compiler_params=params(),
        cost_estimate=pl.CostEstimate(
            flops=slots * 4 * ROWS * C * CELLS, transcendentals=slots * BLK * CELLS, bytes_accessed=slots * 4 * C * CELLS
        ),
    )(scalars, *pieces, w1, w2t)


def call_grads(scalars, pieces, pair):
    slots = pieces[0].shape[1]
    return pl.pallas_call(
        kernel_grads,
        name="weight_grads",
        grid_spec=pltpu.PrefetchScalarGridSpec(
            num_scalar_prefetch=1,
            grid=(slots,),
            in_specs=piece_specs() + [pair_spec()],
            out_specs=[pl.BlockSpec(HALF, lambda s, *_: (0, 0, 0, 0))] * 2,
            scratch_shapes=[
                pltpu.VMEM((C, CELLS), jnp.bfloat16),
                pltpu.VMEM((ROWS, CELLS), jnp.bfloat16),
                pltpu.VMEM((2, C, ROWS), jnp.float32),
            ],
        ),
        out_shape=[jax.ShapeDtypeStruct(HALF, jnp.float32)] * 2,
        compiler_params=params(),
        cost_estimate=pl.CostEstimate(
            flops=slots * 4 * ROWS * C * CELLS, transcendentals=0, bytes_accessed=slots * 4 * C * CELLS
        ),
    )(scalars, *pieces, pair)


def call_two(scalars, pieces, w2, w1t):
    slots = pieces[0].shape[1]
    flat = jax.ShapeDtypeStruct((slots, BLK, CELLS), jnp.float32)
    return pl.pallas_call(
        kernel_two,
        name="layer_two",
        grid_spec=pltpu.PrefetchScalarGridSpec(
            num_scalar_prefetch=1,
            grid=(slots,),
            in_specs=piece_specs() + weight_specs(),
            out_specs=[slot_spec(), slot_spec()],
            scratch_shapes=[
                pltpu.VMEM((C, CELLS), jnp.bfloat16),
                pltpu.VMEM((C, CELLS), jnp.bfloat16),
            ],
        ),
        out_shape=[flat, flat],
        compiler_params=params(),
        cost_estimate=pl.CostEstimate(
            flops=slots * 4 * ROWS * C * CELLS, transcendentals=0, bytes_accessed=slots * 4 * C * CELLS
        ),
    )(scalars, *pieces, w2, w1t)


def kernel_split(scalars, w1, w2, out_ref):
    lane = lax.broadcasted_iota(jnp.int32, (BLK, 128), 1) >> 4

    def split(w):
        for half in range(2):
            for low in range(0, TAPS, 8):
                taps = range(low, min(low + 8, TAPS))
                tiles = [w[t, :, half * 128:(half + 1) * 128].astype(jnp.float32) for t in taps]
                for a in range(8):
                    total = None
                    for j, tile in enumerate(tiles):
                        amount = (BLK * (j - a)) % 128
                        moved = pltpu.roll(tile, amount, 1) if amount else tile
                        total = moved if total is None else jnp.where(lane == j, moved, total)
                    width = BLK * len(tiles)
                    out_ref[half * 8 + a, :, low * BLK:low * BLK + width] = total[:, :width].astype(jnp.bfloat16)

    @pl.when(scalars[3] == 0)
    def _():
        split(w1)

    @pl.when(scalars[3] == 1)
    def _():
        split(w2)


def split_weights(scalars, w1, w2):
    whole = pl.BlockSpec((TAPS, BLK, C), lambda i, *_: (0, 0, 0))
    return pl.pallas_call(
        kernel_split,
        name="split_weights",
        grid_spec=pltpu.PrefetchScalarGridSpec(
            num_scalar_prefetch=1,
            grid=(1,),
            in_specs=[whole, whole],
            out_specs=pl.BlockSpec((BLK, BLK, ROWS), lambda i, *_: (0, 0, 0)),
        ),
        out_shape=jax.ShapeDtypeStruct((BLK, BLK, ROWS), jnp.bfloat16),
        cost_estimate=pl.CostEstimate(flops=0, transcendentals=0, bytes_accessed=4 * ROWS * C * 2),
    )(scalars, w1, w2)


def kernel_collect(mine, got, out_ref):
    lane = lax.broadcasted_iota(jnp.int32, (BLK, 128), 1) >> 4
    flipped = got[...].T
    wide = jnp.concatenate([flipped, jnp.zeros((ROWS, 128 - BLK), jnp.float32)], axis=1)
    out_ref[0] = mine[...]
    for low in range(0, TAPS, 8):
        total = None
        count = min(8, TAPS - low)
        for j in range(count):
            tile = wide[(low + j) * BLK:(low + j + 1) * BLK, :]
            moved = pltpu.roll(tile, BLK * j, 1) if j else tile
            total = moved if total is None else jnp.where(lane == j, moved, total)
        width = BLK * count
        out_ref[1, :, low * BLK:low * BLK + width] = total[:, :width]


def collect(mine, got):
    return pl.pallas_call(
        kernel_collect,
        name="collect_rows",
        out_shape=jax.ShapeDtypeStruct((2, BLK, ROWS), jnp.float32),
        cost_estimate=pl.CostEstimate(flops=0, transcendentals=0, bytes_accessed=16 * ROWS * BLK),
    )(mine, got)


def kernel_finish(rows, first_ref, second_ref, full):
    scale = 1.0 / (BLK * CELLS) ** 0.5
    for k, out_ref in enumerate((first_ref, second_ref)):
        for d in range(BLK):
            full[d * BLK:(d + 1) * BLK, :] = rows[d, k]
        out_ref[...] = full[...].T * scale


def finish(rows):
    return pl.pallas_call(
        kernel_finish,
        name="finish_gradients",
        out_shape=[jax.ShapeDtypeStruct((ROWS, C), jnp.float32)] * 2,
        scratch_shapes=[pltpu.VMEM((C, ROWS), jnp.float32)],
        cost_estimate=pl.CostEstimate(flops=0, transcendentals=0, bytes_accessed=16 * ROWS * C),
    )(rows)


def swap_cores(v):
    return lax.ppermute(v, "dp", [(d, d ^ 1) for d in range(BLK)])


def over_z(v):
    by_core = [[2 * z + core for z in range(8)] for core in range(2)]
    return lax.all_to_all(v, "dp", 0, 0, axis_index_groups=by_core, tiled=True)


def sum_over_dp(keep, send):
    mine = over_z(keep + swap_cores(send)).sum(axis=0)
    flip = [(d * BLK + f, f * BLK + d) for d in range(BLK) for f in range(BLK)]
    got = lax.ppermute(mine[1], ("dp", "filter"), flip)
    return collect(mine[0], got)


def both_gradients(piece):
    first_grad, second_grad = finish(lax.all_gather(piece, "dp", axis=0))
    return first_grad.reshape(TAPS, BLK, C), second_grad.reshape(TAPS, BLK, C)


def shards(patches, cotangent, first_weight, second_weight, counts):
    me = lax.axis_index("filter")
    core = lax.axis_index("dp") % 2
    scalars = jnp.stack([counts[0], me // SIDE, me % SIDE, core]).astype(jnp.int32)
    split = split_weights(scalars, first_weight, second_weight)
    nears = gather_near(jnp.stack([patches.transpose(1, 0, 2), cotangent.transpose(1, 0, 2)]))
    nears, split = lax.optimization_barrier((nears, split))
    fars = gather_far(nears)

    turned = lax.all_to_all(split, "filter", 0, 0, tiled=True).reshape(C, ROWS)
    pieces = gather_last(fars)
    other = swap_cores(turned)
    w1t = jnp.where(core == 0, turned, other).T
    w2t = jnp.where(core == 0, other, turned).T
    w1 = first_weight.reshape(ROWS, C)
    w2 = second_weight.reshape(ROWS, C)

    pair = call_one(scalars, pieces, w1, w2t)
    nears = gather_near(pair)
    keep, send = call_grads(scalars, pieces, pair)
    nears, keep, send = lax.optimization_barrier((nears, keep, send))
    second_pieces = gather_last(gather_far(nears))
    piece = sum_over_dp(keep, send)
    out, in_grad = call_two(scalars, second_pieces, w2, w1t)
    out, in_grad, piece = lax.optimization_barrier((out, in_grad, piece))
    first_grad, second_grad = both_gradients(piece)
    return (out.transpose(1, 0, 2), in_grad.transpose(1, 0, 2), first_grad, second_grad)


def solution(mesh):
    placed = (
        P("filter", "dp", None),
        P("filter", "dp", None),
        P(None, "filter", None),
        P(None, "filter", None),
        P("dp"),
    )
    return jax.shard_map(
        shards,
        mesh=mesh,
        in_specs=placed,
        out_specs=(
            P("filter", "dp", None),
            P("filter", "dp", None),
            P(None, "filter", None),
            P(None, "filter", None),
        ),
        check_vma=False,
    )
```

```python
import functools

import jax
import jax.numpy as jnp
from jax import lax
from jax.experimental import pallas as pl
from jax.experimental.pallas import tpu as pltpu
from jax.sharding import PartitionSpec as P

PX = 8
PY = 16
PZ = 16
CAP = 3
CELLS = 2048
PLANE = PY * PZ
C = 256
BLK = 16
TAPS = 27
ROWS = TAPS * BLK

SIDE = 4
HALF = (8, 2, BLK, ROWS)


def axis_masks():
    cell = lax.broadcasted_iota(jnp.int32, (BLK, CELLS), 1)
    pos_y = (cell >> 4) & 15
    pos_z = cell & 15
    in_y = {-1: pos_y > 0, 0: None, 1: pos_y < PY - 1}
    in_z = {-1: pos_z > 0, 0: None, 1: pos_z < PZ - 1}
    return in_y, in_z


def shift_x(v, ox):
    if ox == 0:
        return v
    zero = jnp.zeros((v.shape[0], PLANE), v.dtype)
    if ox > 0:
        return jnp.concatenate([v[:, PLANE:], zero], axis=1)
    return jnp.concatenate([zero, v[:, :-PLANE]], axis=1)


def shift_yz(v, oy, oz, masks):
    step = oy * PZ + oz
    if step == 0:
        return v
    v = pltpu.roll(v, (-step) % CELLS, 1)
    for inside in (masks[0][oy], masks[1][oz]):
        if inside is not None:
            v = jnp.where(inside, v, 0.0)
    return v


def tap_conv(w_ref, full, sign, masks):
    proj = [
        jnp.dot(w_ref[k * 9 * BLK:(k + 1) * 9 * BLK, :], full, preferred_element_type=jnp.float32)
        for k in range(3)
    ]
    total = None
    for oy in (-1, 0, 1):
        for oz in (-1, 0, 1):
            at = (3 * (oy + 1) + oz + 1) * BLK
            part = None
            for ox in (-1, 0, 1):
                term = shift_x(proj[ox + 1][at:at + BLK, :], sign * ox)
                part = term if part is None else part + term
            part = shift_yz(part, sign * oy, sign * oz, masks)
            total = part if total is None else total + part
    return total


def tap_stack(stack_ref, v, sign, masks):
    for oy in (-1, 0, 1):
        for oz in (-1, 0, 1):
            moved = shift_yz(v, sign * oy, sign * oz, masks)
            for ox in (-1, 0, 1):
                t = 9 * (ox + 1) + 3 * (oy + 1) + (oz + 1)
                stack_ref[t * BLK:(t + 1) * BLK, :] = shift_x(moved, sign * ox).astype(jnp.bfloat16)


def place(scalars, pieces, full_ref, sign):
    x, y, core = scalars[1], scalars[2], scalars[3]
    for outer in range(SIDE):
        for inner in range(SIDE):
            far, near = SIDE + sign * outer, SIDE + inner
            bx = x + jnp.where(core == 0, far, near)
            by = y + jnp.where(core == 0, near, far)
            block = lax.rem(bx, SIDE) * SIDE + lax.rem(by, SIDE)
            at = pl.multiple_of(block * BLK, BLK)
            full_ref[pl.ds(at, BLK), :] = pieces[outer][inner, 0]


def over_cells(a, b):
    return lax.dot_general(a, b, (((1,), (1,)), ((), ())), preferred_element_type=jnp.float32)


def kernel_one(scalars, *refs):
    px, gx = refs[0:4], refs[4:8]
    w1, w2t, pair_out, full_p, full_g = refs[8:]
    s = pl.program_id(0)

    @pl.when(s >= scalars[0])
    def _():
        pair_out[...] = jnp.zeros_like(pair_out)

    @pl.when(s < scalars[0])
    def _():
        masks = axis_masks()
        place(scalars, px, full_p, 1)
        place(scalars, gx, full_g, -1)
        first = tap_conv(w1, full_p[...], 1, masks)
        hidden_grad = tap_conv(w2t, full_g[...], -1, masks)
        sigma = 1.0 / (1.0 + jnp.exp(-first))
        pair_out[0, 0] = (first * sigma).astype(jnp.bfloat16)
        pair_out[1, 0] = (hidden_grad * sigma * (1.0 + first * (1.0 - sigma))).astype(jnp.bfloat16)


def kernel_grads(scalars, *refs):
    px, gx = refs[0:4], refs[4:8]
    pair, keep_out, send_out, full, stack, grads = refs[8:]
    s = pl.program_id(0)
    core = scalars[3]

    @pl.when(s == 0)
    def _():
        grads[...] = jnp.zeros_like(grads)

    @pl.when(s < scalars[0])
    def _():
        masks = axis_masks()
        place(scalars, px, full, 1)
        tap_stack(stack, pair[1, 0].astype(jnp.float32), -1, masks)
        grads[0] += over_cells(full[...], stack[...])
        place(scalars, gx, full, -1)
        tap_stack(stack, pair[0, 0].astype(jnp.float32), 1, masks)
        grads[1] += over_cells(full[...], stack[...])

    @pl.when(s == pl.num_programs(0) - 1)
    def _():
        for z in range(8):
            for k in range(2):
                keep_out[z, k] = grads[k, pl.ds(pl.multiple_of((2 * z + core) * BLK, BLK), BLK), :]
                send_out[z, k] = grads[k, pl.ds(pl.multiple_of((2 * z + 1 - core) * BLK, BLK), BLK), :]


def kernel_two(scalars, *refs):
    hx, dx = refs[0:4], refs[4:8]
    w2, w1t, out_ref, in_ref, full_h, full_d = refs[8:]
    s = pl.program_id(0)

    @pl.when(s >= scalars[0])
    def _():
        out_ref[...] = jnp.zeros_like(out_ref)
        in_ref[...] = jnp.zeros_like(in_ref)

    @pl.when(s < scalars[0])
    def _():
        masks = axis_masks()
        place(scalars, hx, full_h, 1)
        place(scalars, dx, full_d, -1)
        out_ref[0] = tap_conv(w2, full_h[...], 1, masks)
        in_ref[0] = tap_conv(w1t, full_d[...], -1, masks)


def from_axis(axes, step):
    pairs = []
    for d in range(BLK):
        for x in range(SIDE):
            for y in range(SIDE):
                sx, sy = (x + step, y) if axes[d % 2] == "x" else (x, y + step)
                pairs.append((d * BLK + (sx % SIDE) * SIDE + sy % SIDE, d * BLK + x * SIDE + y))
    return pairs


def turn(v, axes, step):
    return lax.ppermute(v, ("dp", "filter"), from_axis(axes, step))


def gather_near(pair):
    near = [pair] + [turn(pair, "yx", k) for k in (1, 2, 3)]
    return [jnp.stack([v[k] for v in near]) for k in range(2)]


def gather_far(nears):
    return [(own, turn(own, "xy", sign), turn(own, "xy", -sign)) for own, sign in zip(nears, (1, -1))]


def gather_last(parts):
    pieces = []
    for (own, ahead, behind), sign in zip(parts, (1, -1)):
        pieces += [own, ahead, turn(ahead, "xy", sign), behind]
    return pieces


def live_slot(s, scalars):
    return jnp.minimum(s, jnp.maximum(scalars[0] - 1, 0))


def piece_specs():
    return [pl.BlockSpec((SIDE, 1, BLK, CELLS), lambda s, sc: (0, live_slot(s, sc), 0, 0))] * 8


def weight_specs():
    return [pl.BlockSpec((ROWS, C), lambda s, *_: (0, 0))] * 2


def slot_spec():
    return pl.BlockSpec((1, BLK, CELLS), lambda s, *_: (s, 0, 0))


def pair_spec():
    return pl.BlockSpec((2, 1, BLK, CELLS), lambda s, *_: (0, s, 0, 0))


def params():
    return pltpu.CompilerParams(vmem_limit_bytes=48 * 1024 * 1024)


def call_one(scalars, pieces, w1, w2t):
    slots = pieces[0].shape[1]
    pair = jax.ShapeDtypeStruct((2, slots, BLK, CELLS), jnp.bfloat16)
    return pl.pallas_call(
        kernel_one,
        name="layer_one",
        grid_spec=pltpu.PrefetchScalarGridSpec(
            num_scalar_prefetch=1,
            grid=(slots,),
            in_specs=piece_specs() + weight_specs(),
            out_specs=pair_spec(),
            scratch_shapes=[pltpu.VMEM((C, CELLS), jnp.bfloat16)] * 2,
        ),
        out_shape=pair,
        compiler_params=params(),
        cost_estimate=pl.CostEstimate(
            flops=slots * 4 * ROWS * C * CELLS, transcendentals=slots * BLK * CELLS, bytes_accessed=slots * 4 * C * CELLS
        ),
    )(scalars, *pieces, w1, w2t)


def call_grads(scalars, pieces, pair):
    slots = pieces[0].shape[1]
    return pl.pallas_call(
        kernel_grads,
        name="weight_grads",
        grid_spec=pltpu.PrefetchScalarGridSpec(
            num_scalar_prefetch=1,
            grid=(slots,),
            in_specs=piece_specs() + [pair_spec()],
            out_specs=[pl.BlockSpec(HALF, lambda s, *_: (0, 0, 0, 0))] * 2,
            scratch_shapes=[
                pltpu.VMEM((C, CELLS), jnp.bfloat16),
                pltpu.VMEM((ROWS, CELLS), jnp.bfloat16),
                pltpu.VMEM((2, C, ROWS), jnp.float32),
            ],
        ),
        out_shape=[jax.ShapeDtypeStruct(HALF, jnp.float32)] * 2,
        compiler_params=params(),
        cost_estimate=pl.CostEstimate(
            flops=slots * 4 * ROWS * C * CELLS, transcendentals=0, bytes_accessed=slots * 4 * C * CELLS
        ),
    )(scalars, *pieces, pair)


def call_two(scalars, pieces, w2, w1t):
    slots = pieces[0].shape[1]
    flat = jax.ShapeDtypeStruct((slots, BLK, CELLS), jnp.float32)
    return pl.pallas_call(
        kernel_two,
        name="layer_two",
        grid_spec=pltpu.PrefetchScalarGridSpec(
            num_scalar_prefetch=1,
            grid=(slots,),
            in_specs=piece_specs() + weight_specs(),
            out_specs=[slot_spec(), slot_spec()],
            scratch_shapes=[
                pltpu.VMEM((C, CELLS), jnp.bfloat16),
                pltpu.VMEM((C, CELLS), jnp.bfloat16),
            ],
        ),
        out_shape=[flat, flat],
        compiler_params=params(),
        cost_estimate=pl.CostEstimate(
            flops=slots * 4 * ROWS * C * CELLS, transcendentals=0, bytes_accessed=slots * 4 * C * CELLS
        ),
    )(scalars, *pieces, w2, w1t)


def kernel_split(scalars, w1, w2, out_ref):
    lane = lax.broadcasted_iota(jnp.int32, (BLK, 128), 1) >> 4

    def split(w):
        for half in range(2):
            for low in range(0, TAPS, 8):
                taps = range(low, min(low + 8, TAPS))
                tiles = [w[t, :, half * 128:(half + 1) * 128].astype(jnp.float32) for t in taps]
                for a in range(8):
                    total = None
                    for j, tile in enumerate(tiles):
                        amount = (BLK * (j - a)) % 128
                        moved = pltpu.roll(tile, amount, 1) if amount else tile
                        total = moved if total is None else jnp.where(lane == j, moved, total)
                    width = BLK * len(tiles)
                    out_ref[half * 8 + a, :, low * BLK:low * BLK + width] = total[:, :width].astype(jnp.bfloat16)

    @pl.when(scalars[3] == 0)
    def _():
        split(w1)

    @pl.when(scalars[3] == 1)
    def _():
        split(w2)


def split_weights(scalars, w1, w2):
    whole = pl.BlockSpec((TAPS, BLK, C), lambda i, *_: (0, 0, 0))
    return pl.pallas_call(
        kernel_split,
        name="split_weights",
        grid_spec=pltpu.PrefetchScalarGridSpec(
            num_scalar_prefetch=1,
            grid=(1,),
            in_specs=[whole, whole],
            out_specs=pl.BlockSpec((BLK, BLK, ROWS), lambda i, *_: (0, 0, 0)),
        ),
        out_shape=jax.ShapeDtypeStruct((BLK, BLK, ROWS), jnp.bfloat16),
        cost_estimate=pl.CostEstimate(flops=0, transcendentals=0, bytes_accessed=4 * ROWS * C * 2),
    )(scalars, w1, w2)


def kernel_collect(mine, got, out_ref):
    lane = lax.broadcasted_iota(jnp.int32, (BLK, 128), 1) >> 4
    flipped = got[...].T
    wide = jnp.concatenate([flipped, jnp.zeros((ROWS, 128 - BLK), jnp.float32)], axis=1)
    out_ref[0] = mine[...]
    for low in range(0, TAPS, 8):
        total = None
        count = min(8, TAPS - low)
        for j in range(count):
            tile = wide[(low + j) * BLK:(low + j + 1) * BLK, :]
            moved = pltpu.roll(tile, BLK * j, 1) if j else tile
            total = moved if total is None else jnp.where(lane == j, moved, total)
        width = BLK * count
        out_ref[1, :, low * BLK:low * BLK + width] = total[:, :width]


def collect(mine, got):
    return pl.pallas_call(
        kernel_collect,
        name="collect_rows",
        out_shape=jax.ShapeDtypeStruct((2, BLK, ROWS), jnp.float32),
        cost_estimate=pl.CostEstimate(flops=0, transcendentals=0, bytes_accessed=16 * ROWS * BLK),
    )(mine, got)


def kernel_finish(rows, first_ref, second_ref, full):
    scale = 1.0 / (BLK * CELLS) ** 0.5
    for k, out_ref in enumerate((first_ref, second_ref)):
        for d in range(BLK):
            full[d * BLK:(d + 1) * BLK, :] = rows[d, k]
        out_ref[...] = full[...].T * scale


def finish(rows):
    return pl.pallas_call(
        kernel_finish,
        name="finish_gradients",
        out_shape=[jax.ShapeDtypeStruct((ROWS, C), jnp.float32)] * 2,
        scratch_shapes=[pltpu.VMEM((C, ROWS), jnp.float32)],
        cost_estimate=pl.CostEstimate(flops=0, transcendentals=0, bytes_accessed=16 * ROWS * C),
    )(rows)


def swap_cores(v):
    return lax.ppermute(v, "dp", [(d, d ^ 1) for d in range(BLK)])


def over_z(v):
    by_core = [[2 * z + core for z in range(8)] for core in range(2)]
    return lax.all_to_all(v, "dp", 0, 0, axis_index_groups=by_core, tiled=True)


def sum_over_dp(parts, done):
    mine = parts.astype(jnp.float32).sum(axis=0)
    flip = [(d * BLK + f, f * BLK + d) for d in range(BLK) for f in range(BLK)]
    got = lax.ppermute(mine[1], ("dp", "filter"), flip)
    got, done = lax.optimization_barrier((got, done))
    return collect(mine[0], got), done


def both_gradients(piece):
    first_grad, second_grad = finish(lax.all_gather(piece, "dp", axis=0))
    return first_grad.reshape(TAPS, BLK, C), second_grad.reshape(TAPS, BLK, C)


def shards(patches, cotangent, first_weight, second_weight, counts):
    me = lax.axis_index("filter")
    core = lax.axis_index("dp") % 2
    scalars = jnp.stack([counts[0], me // SIDE, me % SIDE, core]).astype(jnp.int32)
    split = split_weights(scalars, first_weight, second_weight)
    nears = gather_near(jnp.stack([patches.transpose(1, 0, 2), cotangent.transpose(1, 0, 2)]))
    nears, split = lax.optimization_barrier((nears, split))
    fars = gather_far(nears)

    turned = lax.all_to_all(split, "filter", 0, 0, tiled=True).reshape(C, ROWS)
    pieces = gather_last(fars)
    other = swap_cores(turned)
    w1t = jnp.where(core == 0, turned, other).T
    w2t = jnp.where(core == 0, other, turned).T
    w1 = first_weight.reshape(ROWS, C)
    w2 = second_weight.reshape(ROWS, C)

    pair = call_one(scalars, pieces, w1, w2t)
    nears = gather_near(pair)
    keep, send = call_grads(scalars, pieces, pair)
    pair_sum = (keep + swap_cores(send)).astype(jnp.bfloat16)
    nears, pair_sum = lax.optimization_barrier((nears, pair_sum))
    fars = gather_far(nears)
    parts = over_z(pair_sum)
    fars[0], parts = lax.optimization_barrier((fars[0], parts))
    second_pieces = gather_last(fars)
    out, in_grad = call_two(scalars, second_pieces, w2, w1t)
    piece, (out, in_grad) = sum_over_dp(parts, (out, in_grad))
    first_grad, second_grad = both_gradients(piece)
    return (out.transpose(1, 0, 2), in_grad.transpose(1, 0, 2), first_grad, second_grad)


def solution(mesh):
    placed = (
        P("filter", "dp", None),
        P("filter", "dp", None),
        P(None, "filter", None),
        P(None, "filter", None),
        P("dp"),
    )
    return jax.shard_map(
        shards,
        mesh=mesh,
        in_specs=placed,
        out_specs=(
            P("filter", "dp", None),
            P("filter", "dp", None),
            P(None, "filter", None),
            P(None, "filter", None),
        ),
        check_vma=False,
    )
```

```python
import functools

import jax
import jax.numpy as jnp
from jax import lax
from jax.experimental import pallas as pl
from jax.experimental.pallas import tpu as pltpu
from jax.sharding import PartitionSpec as P

PX = 8
PY = 16
PZ = 16
CAP = 3
CELLS = 2048
PLANE = PY * PZ
C = 256
BLK = 16
TAPS = 27
ROWS = TAPS * BLK

SIDE = 4
HALF = (8, 2, BLK, ROWS)


def axis_masks():
    cell = lax.broadcasted_iota(jnp.int32, (BLK, CELLS), 1)
    pos_y = (cell >> 4) & 15
    pos_z = cell & 15
    in_y = {-1: pos_y > 0, 0: None, 1: pos_y < PY - 1}
    in_z = {-1: pos_z > 0, 0: None, 1: pos_z < PZ - 1}
    return in_y, in_z


def shift_x(v, ox):
    if ox == 0:
        return v
    zero = jnp.zeros((v.shape[0], PLANE), v.dtype)
    if ox > 0:
        return jnp.concatenate([v[:, PLANE:], zero], axis=1)
    return jnp.concatenate([zero, v[:, :-PLANE]], axis=1)


def shift_yz(v, oy, oz, masks):
    step = oy * PZ + oz
    if step == 0:
        return v
    v = pltpu.roll(v, (-step) % CELLS, 1)
    for inside in (masks[0][oy], masks[1][oz]):
        if inside is not None:
            v = jnp.where(inside, v, 0.0)
    return v


def tap_conv(w_ref, full, sign, masks):
    proj = [
        jnp.dot(w_ref[k * 9 * BLK:(k + 1) * 9 * BLK, :], full, preferred_element_type=jnp.float32)
        for k in range(3)
    ]
    total = None
    for oy in (-1, 0, 1):
        for oz in (-1, 0, 1):
            at = (3 * (oy + 1) + oz + 1) * BLK
            part = None
            for ox in (-1, 0, 1):
                term = shift_x(proj[ox + 1][at:at + BLK, :], sign * ox)
                part = term if part is None else part + term
            part = shift_yz(part, sign * oy, sign * oz, masks)
            total = part if total is None else total + part
    return total


def tap_stack(stack_ref, v, sign, masks):
    for oy in (-1, 0, 1):
        for oz in (-1, 0, 1):
            moved = shift_yz(v, sign * oy, sign * oz, masks)
            for ox in (-1, 0, 1):
                t = 9 * (ox + 1) + 3 * (oy + 1) + (oz + 1)
                stack_ref[t * BLK:(t + 1) * BLK, :] = shift_x(moved, sign * ox).astype(jnp.bfloat16)


def place(scalars, pieces, full_ref, sign):
    x, y, core = scalars[1], scalars[2], scalars[3]
    for outer in range(SIDE):
        for inner in range(SIDE):
            far, near = SIDE + sign * outer, SIDE + inner
            bx = x + jnp.where(core == 0, far, near)
            by = y + jnp.where(core == 0, near, far)
            block = lax.rem(bx, SIDE) * SIDE + lax.rem(by, SIDE)
            at = pl.multiple_of(block * BLK, BLK)
            full_ref[pl.ds(at, BLK), :] = pieces[outer][inner, 0]


def over_cells(a, b):
    return lax.dot_general(a, b, (((1,), (1,)), ((), ())), preferred_element_type=jnp.float32)


def kernel_one(scalars, *refs):
    px, gx = refs[0:4], refs[4:8]
    w1, w2t, pair_out, full_p, full_g = refs[8:]
    s = pl.program_id(0)

    @pl.when(s >= scalars[0])
    def _():
        pair_out[...] = jnp.zeros_like(pair_out)

    @pl.when(s < scalars[0])
    def _():
        masks = axis_masks()
        place(scalars, px, full_p, 1)
        place(scalars, gx, full_g, -1)
        first = tap_conv(w1, full_p[...], 1, masks)
        hidden_grad = tap_conv(w2t, full_g[...], -1, masks)
        sigma = 1.0 / (1.0 + jnp.exp(-first))
        pair_out[0, 0] = (first * sigma).astype(jnp.bfloat16)
        pair_out[1, 0] = (hidden_grad * sigma * (1.0 + first * (1.0 - sigma))).astype(jnp.bfloat16)


def kernel_grads(scalars, *refs):
    px, gx = refs[0:4], refs[4:8]
    pair, keep_out, send_out, full, stack, grads = refs[8:]
    s = pl.program_id(0)
    core = scalars[3]

    @pl.when(s == 0)
    def _():
        grads[...] = jnp.zeros_like(grads)

    @pl.when(s < scalars[0])
    def _():
        masks = axis_masks()
        place(scalars, px, full, 1)
        tap_stack(stack, pair[1, 0].astype(jnp.float32), -1, masks)
        grads[0] += over_cells(full[...], stack[...])
        place(scalars, gx, full, -1)
        tap_stack(stack, pair[0, 0].astype(jnp.float32), 1, masks)
        grads[1] += over_cells(full[...], stack[...])

    @pl.when(s == pl.num_programs(0) - 1)
    def _():
        for z in range(8):
            for k in range(2):
                keep_out[z, k] = grads[k, pl.ds(pl.multiple_of((2 * z + core) * BLK, BLK), BLK), :]
                send_out[z, k] = grads[k, pl.ds(pl.multiple_of((2 * z + 1 - core) * BLK, BLK), BLK), :]


def kernel_two(scalars, *refs):
    hx, dx = refs[0:4], refs[4:8]
    w2, w1t, out_ref, in_ref, full_h, full_d = refs[8:]
    s = pl.program_id(0)

    @pl.when(s >= scalars[0])
    def _():
        out_ref[...] = jnp.zeros_like(out_ref)
        in_ref[...] = jnp.zeros_like(in_ref)

    @pl.when(s < scalars[0])
    def _():
        masks = axis_masks()
        place(scalars, hx, full_h, 1)
        place(scalars, dx, full_d, -1)
        out_ref[0] = tap_conv(w2, full_h[...], 1, masks)
        in_ref[0] = tap_conv(w1t, full_d[...], -1, masks)


def from_axis(axes, step):
    pairs = []
    for d in range(BLK):
        for x in range(SIDE):
            for y in range(SIDE):
                sx, sy = (x + step, y) if axes[d % 2] == "x" else (x, y + step)
                pairs.append((d * BLK + (sx % SIDE) * SIDE + sy % SIDE, d * BLK + x * SIDE + y))
    return pairs


def turn(v, axes, step):
    return lax.ppermute(v, ("dp", "filter"), from_axis(axes, step))


def gather_near(pair):
    near = [pair] + [turn(pair, "yx", k) for k in (1, 2, 3)]
    return [jnp.stack([v[k] for v in near]) for k in range(2)]


def gather_far(nears):
    return [(own, turn(own, "xy", sign), turn(own, "xy", -sign)) for own, sign in zip(nears, (1, -1))]


def gather_last(parts):
    pieces = []
    for (own, ahead, behind), sign in zip(parts, (1, -1)):
        pieces += [own, ahead, turn(ahead, "xy", sign), behind]
    return pieces


def live_slot(s, scalars):
    return jnp.minimum(s, jnp.maximum(scalars[0] - 1, 0))


def piece_specs():
    return [pl.BlockSpec((SIDE, 1, BLK, CELLS), lambda s, sc: (0, live_slot(s, sc), 0, 0))] * 8


def weight_specs():
    return [pl.BlockSpec((ROWS, C), lambda s, *_: (0, 0))] * 2


def slot_spec():
    return pl.BlockSpec((1, BLK, CELLS), lambda s, *_: (s, 0, 0))


def pair_spec():
    return pl.BlockSpec((2, 1, BLK, CELLS), lambda s, *_: (0, s, 0, 0))


def params():
    return pltpu.CompilerParams(vmem_limit_bytes=48 * 1024 * 1024)


def call_one(scalars, pieces, w1, w2t):
    slots = pieces[0].shape[1]
    pair = jax.ShapeDtypeStruct((2, slots, BLK, CELLS), jnp.bfloat16)
    return pl.pallas_call(
        kernel_one,
        name="layer_one",
        grid_spec=pltpu.PrefetchScalarGridSpec(
            num_scalar_prefetch=1,
            grid=(slots,),
            in_specs=piece_specs() + weight_specs(),
            out_specs=pair_spec(),
            scratch_shapes=[pltpu.VMEM((C, CELLS), jnp.bfloat16)] * 2,
        ),
        out_shape=pair,
        compiler_params=params(),
        cost_estimate=pl.CostEstimate(
            flops=slots * 4 * ROWS * C * CELLS, transcendentals=slots * BLK * CELLS, bytes_accessed=slots * 4 * C * CELLS
        ),
    )(scalars, *pieces, w1, w2t)


def call_grads(scalars, pieces, pair):
    slots = pieces[0].shape[1]
    return pl.pallas_call(
        kernel_grads,
        name="weight_grads",
        grid_spec=pltpu.PrefetchScalarGridSpec(
            num_scalar_prefetch=1,
            grid=(slots,),
            in_specs=piece_specs() + [pair_spec()],
            out_specs=[pl.BlockSpec(HALF, lambda s, *_: (0, 0, 0, 0))] * 2,
            scratch_shapes=[
                pltpu.VMEM((C, CELLS), jnp.bfloat16),
                pltpu.VMEM((ROWS, CELLS), jnp.bfloat16),
                pltpu.VMEM((2, C, ROWS), jnp.float32),
            ],
        ),
        out_shape=[jax.ShapeDtypeStruct(HALF, jnp.float32)] * 2,
        compiler_params=params(),
        cost_estimate=pl.CostEstimate(
            flops=slots * 4 * ROWS * C * CELLS, transcendentals=0, bytes_accessed=slots * 4 * C * CELLS
        ),
    )(scalars, *pieces, pair)


def call_two(scalars, pieces, w2, w1t):
    slots = pieces[0].shape[1]
    flat = jax.ShapeDtypeStruct((slots, BLK, CELLS), jnp.float32)
    return pl.pallas_call(
        kernel_two,
        name="layer_two",
        grid_spec=pltpu.PrefetchScalarGridSpec(
            num_scalar_prefetch=1,
            grid=(slots,),
            in_specs=piece_specs() + weight_specs(),
            out_specs=[slot_spec(), slot_spec()],
            scratch_shapes=[
                pltpu.VMEM((C, CELLS), jnp.bfloat16),
                pltpu.VMEM((C, CELLS), jnp.bfloat16),
            ],
        ),
        out_shape=[flat, flat],
        compiler_params=params(),
        cost_estimate=pl.CostEstimate(
            flops=slots * 4 * ROWS * C * CELLS, transcendentals=0, bytes_accessed=slots * 4 * C * CELLS
        ),
    )(scalars, *pieces, w2, w1t)


def kernel_split(scalars, w1, w2, out_ref):
    lane = lax.broadcasted_iota(jnp.int32, (BLK, 128), 1) >> 4

    def split(w):
        for half in range(2):
            for low in range(0, TAPS, 8):
                taps = range(low, min(low + 8, TAPS))
                tiles = [w[t, :, half * 128:(half + 1) * 128].astype(jnp.float32) for t in taps]
                for a in range(8):
                    total = None
                    for j, tile in enumerate(tiles):
                        amount = (BLK * (j - a)) % 128
                        moved = pltpu.roll(tile, amount, 1) if amount else tile
                        total = moved if total is None else jnp.where(lane == j, moved, total)
                    width = BLK * len(tiles)
                    out_ref[half * 8 + a, :, low * BLK:low * BLK + width] = total[:, :width].astype(jnp.bfloat16)

    @pl.when(scalars[3] == 0)
    def _():
        split(w1)

    @pl.when(scalars[3] == 1)
    def _():
        split(w2)


def split_weights(scalars, w1, w2):
    whole = pl.BlockSpec((TAPS, BLK, C), lambda i, *_: (0, 0, 0))
    return pl.pallas_call(
        kernel_split,
        name="split_weights",
        grid_spec=pltpu.PrefetchScalarGridSpec(
            num_scalar_prefetch=1,
            grid=(1,),
            in_specs=[whole, whole],
            out_specs=pl.BlockSpec((BLK, BLK, ROWS), lambda i, *_: (0, 0, 0)),
        ),
        out_shape=jax.ShapeDtypeStruct((BLK, BLK, ROWS), jnp.bfloat16),
        cost_estimate=pl.CostEstimate(flops=0, transcendentals=0, bytes_accessed=4 * ROWS * C * 2),
    )(scalars, w1, w2)


def kernel_collect(mine, got, out_ref):
    lane = lax.broadcasted_iota(jnp.int32, (BLK, 128), 1) >> 4
    flipped = got[...].T
    wide = jnp.concatenate([flipped, jnp.zeros((ROWS, 128 - BLK), jnp.float32)], axis=1)
    for z in range(8):
        out_ref[z, 0] = mine[...]
    for low in range(0, TAPS, 8):
        total = None
        count = min(8, TAPS - low)
        for j in range(count):
            tile = wide[(low + j) * BLK:(low + j + 1) * BLK, :]
            moved = pltpu.roll(tile, BLK * j, 1) if j else tile
            total = moved if total is None else jnp.where(lane == j, moved, total)
        width = BLK * count
        for z in range(8):
            out_ref[z, 1, :, low * BLK:low * BLK + width] = total[:, :width]


def collect(mine, got):
    return pl.pallas_call(
        kernel_collect,
        name="collect_rows",
        out_shape=jax.ShapeDtypeStruct(HALF, jnp.float32),
        cost_estimate=pl.CostEstimate(flops=0, transcendentals=0, bytes_accessed=4 * ROWS * C),
    )(mine, got)


def kernel_finish(scalars, own, other, first_ref, second_ref, full):
    core = scalars[3]
    scale = 1.0 / (BLK * CELLS) ** 0.5
    for k, out_ref in enumerate((first_ref, second_ref)):
        for z in range(8):
            full[pl.ds(pl.multiple_of((2 * z + core) * BLK, BLK), BLK), :] = own[z, k]
            full[pl.ds(pl.multiple_of((2 * z + 1 - core) * BLK, BLK), BLK), :] = other[z, k]
        out_ref[...] = full[...].T * scale


def finish(scalars, own, other):
    half = pl.BlockSpec(HALF, lambda i, *_: (0, 0, 0, 0))
    turned = pl.BlockSpec((ROWS, C), lambda i, *_: (0, 0))
    return pl.pallas_call(
        kernel_finish,
        name="finish_gradients",
        grid_spec=pltpu.PrefetchScalarGridSpec(
            num_scalar_prefetch=1,
            grid=(1,),
            in_specs=[half, half],
            out_specs=[turned, turned],
            scratch_shapes=[pltpu.VMEM((C, ROWS), jnp.float32)],
        ),
        out_shape=[jax.ShapeDtypeStruct((ROWS, C), jnp.float32)] * 2,
        cost_estimate=pl.CostEstimate(flops=0, transcendentals=0, bytes_accessed=16 * ROWS * C),
    )(scalars, own, other)


def swap_cores(v):
    return lax.ppermute(v, "dp", [(d, d ^ 1) for d in range(BLK)])


def over_z(v):
    by_core = [[2 * z + core for z in range(8)] for core in range(2)]
    return lax.all_to_all(v, "dp", 0, 0, axis_index_groups=by_core, tiled=True)


def sum_over_dp(parts):
    mine = parts.astype(jnp.float32).sum(axis=0)
    flip = [(d * BLK + f, f * BLK + d) for d in range(BLK) for f in range(BLK)]
    got = lax.ppermute(mine[1], ("dp", "filter"), flip)
    return over_z(collect(mine[0], got))


def both_gradients(scalars, own):
    first_grad, second_grad = finish(scalars, own, swap_cores(own))
    return first_grad.reshape(TAPS, BLK, C), second_grad.reshape(TAPS, BLK, C)


def shards(patches, cotangent, first_weight, second_weight, counts):
    me = lax.axis_index("filter")
    core = lax.axis_index("dp") % 2
    scalars = jnp.stack([counts[0], me // SIDE, me % SIDE, core]).astype(jnp.int32)
    split = split_weights(scalars, first_weight, second_weight)
    nears = gather_near(jnp.stack([patches.transpose(1, 0, 2), cotangent.transpose(1, 0, 2)]))
    nears, split = lax.optimization_barrier((nears, split))
    fars = gather_far(nears)

    turned = lax.all_to_all(split, "filter", 0, 0, tiled=True).reshape(C, ROWS)
    pieces = gather_last(fars)
    other = swap_cores(turned)
    w1t = jnp.where(core == 0, turned, other).T
    w2t = jnp.where(core == 0, other, turned).T
    w1 = first_weight.reshape(ROWS, C)
    w2 = second_weight.reshape(ROWS, C)

    pair = call_one(scalars, pieces, w1, w2t)
    nears = gather_near(pair)
    keep, send = call_grads(scalars, pieces, pair)
    pair_sum = (keep + swap_cores(send)).astype(jnp.bfloat16)
    nears, pair_sum = lax.optimization_barrier((nears, pair_sum))
    fars = gather_far(nears)
    parts = over_z(pair_sum)
    fars[0], parts = lax.optimization_barrier((fars[0], parts))
    second_pieces = gather_last(fars)
    own = sum_over_dp(parts)
    out, in_grad = call_two(scalars, second_pieces, w2, w1t)
    out, in_grad, own = lax.optimization_barrier((out, in_grad, own))
    first_grad, second_grad = both_gradients(scalars, own)
    return (out.transpose(1, 0, 2), in_grad.transpose(1, 0, 2), first_grad, second_grad)


def solution(mesh):
    placed = (
        P("filter", "dp", None),
        P("filter", "dp", None),
        P(None, "filter", None),
        P(None, "filter", None),
        P("dp"),
    )
    return jax.shard_map(
        shards,
        mesh=mesh,
        in_specs=placed,
        out_specs=(
            P("filter", "dp", None),
            P("filter", "dp", None),
            P(None, "filter", None),
            P(None, "filter", None),
        ),
        check_vma=False,
    )
```

```python
import functools

import jax
import jax.numpy as jnp
from jax import lax
from jax.experimental import pallas as pl
from jax.experimental.pallas import tpu as pltpu
from jax.sharding import PartitionSpec as P

PX = 8
PY = 16
PZ = 16
CAP = 3
CELLS = 2048
PLANE = PY * PZ
C = 256
BLK = 16
TAPS = 27
ROWS = TAPS * BLK

SIDE = 4
HALF = (8, 2, BLK, ROWS)


def axis_masks():
    cell = lax.broadcasted_iota(jnp.int32, (BLK, CELLS), 1)
    pos_y = (cell >> 4) & 15
    pos_z = cell & 15
    in_y = {-1: pos_y > 0, 0: None, 1: pos_y < PY - 1}
    in_z = {-1: pos_z > 0, 0: None, 1: pos_z < PZ - 1}
    return in_y, in_z


def shift_x(v, ox):
    if ox == 0:
        return v
    zero = jnp.zeros((v.shape[0], PLANE), v.dtype)
    if ox > 0:
        return jnp.concatenate([v[:, PLANE:], zero], axis=1)
    return jnp.concatenate([zero, v[:, :-PLANE]], axis=1)


def shift_yz(v, oy, oz, masks):
    step = oy * PZ + oz
    if step == 0:
        return v
    v = pltpu.roll(v, (-step) % CELLS, 1)
    for inside in (masks[0][oy], masks[1][oz]):
        if inside is not None:
            v = jnp.where(inside, v, 0.0)
    return v


def tap_conv(w_ref, full, sign, masks):
    proj = [
        jnp.dot(w_ref[k * 9 * BLK:(k + 1) * 9 * BLK, :], full, preferred_element_type=jnp.float32)
        for k in range(3)
    ]
    total = None
    for oy in (-1, 0, 1):
        for oz in (-1, 0, 1):
            at = (3 * (oy + 1) + oz + 1) * BLK
            part = None
            for ox in (-1, 0, 1):
                term = shift_x(proj[ox + 1][at:at + BLK, :], sign * ox)
                part = term if part is None else part + term
            part = shift_yz(part, sign * oy, sign * oz, masks)
            total = part if total is None else total + part
    return total


def tap_stack(stack_ref, v, sign, masks):
    for oy in (-1, 0, 1):
        for oz in (-1, 0, 1):
            moved = shift_yz(v, sign * oy, sign * oz, masks)
            for ox in (-1, 0, 1):
                t = 9 * (ox + 1) + 3 * (oy + 1) + (oz + 1)
                stack_ref[t * BLK:(t + 1) * BLK, :] = shift_x(moved, sign * ox).astype(jnp.bfloat16)


def place(scalars, pieces, full_ref, sign):
    x, y, core = scalars[1], scalars[2], scalars[3]
    for outer in range(SIDE):
        for inner in range(SIDE):
            far, near = SIDE + sign * outer, SIDE + inner
            bx = x + jnp.where(core == 0, far, near)
            by = y + jnp.where(core == 0, near, far)
            block = lax.rem(bx, SIDE) * SIDE + lax.rem(by, SIDE)
            at = pl.multiple_of(block * BLK, BLK)
            full_ref[pl.ds(at, BLK), :] = pieces[outer][inner, 0]


def over_cells(a, b):
    return lax.dot_general(a, b, (((1,), (1,)), ((), ())), preferred_element_type=jnp.float32)


def kernel_one(scalars, *refs):
    px, gx = refs[0:4], refs[4:8]
    w1, first_out, second_out, full, stack = refs[8:]
    s = pl.program_id(0)

    @pl.when(s == 0)
    def _():
        second_out[...] = jnp.zeros_like(second_out)

    @pl.when(s >= scalars[0])
    def _():
        first_out[...] = jnp.zeros_like(first_out)

    @pl.when(s < scalars[0])
    def _():
        masks = axis_masks()
        place(scalars, px, full, 1)
        first = tap_conv(w1, full[...], 1, masks)
        first_out[0] = first
        hidden = (first * (1.0 / (1.0 + jnp.exp(-first)))).astype(jnp.bfloat16)
        place(scalars, gx, full, -1)
        tap_stack(stack, hidden.astype(jnp.float32), 1, masks)
        second_out[...] += over_cells(full[...], stack[...])


def kernel_delta(scalars, *refs):
    gx = refs[0:4]
    w2t, first_in, pair_out, full = refs[4:]
    s = pl.program_id(0)

    @pl.when(s >= scalars[0])
    def _():
        pair_out[...] = jnp.zeros_like(pair_out)

    @pl.when(s < scalars[0])
    def _():
        masks = axis_masks()
        place(scalars, gx, full, -1)
        hidden_grad = tap_conv(w2t, full[...], -1, masks)
        first = first_in[0]
        sigma = 1.0 / (1.0 + jnp.exp(-first))
        pair_out[0, 0] = (first * sigma).astype(jnp.bfloat16)
        pair_out[1, 0] = (hidden_grad * sigma * (1.0 + first * (1.0 - sigma))).astype(jnp.bfloat16)


def kernel_grads(scalars, *refs):
    px = refs[0:4]
    pair, second, keep_out, send_out, full, stack, first_sum = refs[4:]
    s = pl.program_id(0)
    core = scalars[3]

    @pl.when(s == 0)
    def _():
        first_sum[...] = jnp.zeros_like(first_sum)

    @pl.when(s < scalars[0])
    def _():
        masks = axis_masks()
        place(scalars, px, full, 1)
        tap_stack(stack, pair[1, 0].astype(jnp.float32), -1, masks)
        first_sum[...] += over_cells(full[...], stack[...])

    @pl.when(s == pl.num_programs(0) - 1)
    def _():
        for z in range(8):
            for k, total in enumerate((first_sum, second)):
                keep_out[z, k] = total[pl.ds(pl.multiple_of((2 * z + core) * BLK, BLK), BLK), :]
                send_out[z, k] = total[pl.ds(pl.multiple_of((2 * z + 1 - core) * BLK, BLK), BLK), :]


def kernel_two(scalars, *refs):
    hx, dx = refs[0:4], refs[4:8]
    w2, w1t, out_ref, in_ref, full_h, full_d = refs[8:]
    s = pl.program_id(0)

    @pl.when(s >= scalars[0])
    def _():
        out_ref[...] = jnp.zeros_like(out_ref)
        in_ref[...] = jnp.zeros_like(in_ref)

    @pl.when(s < scalars[0])
    def _():
        masks = axis_masks()
        place(scalars, hx, full_h, 1)
        place(scalars, dx, full_d, -1)
        out_ref[0] = tap_conv(w2, full_h[...], 1, masks)
        in_ref[0] = tap_conv(w1t, full_d[...], -1, masks)


def from_axis(axes, step):
    pairs = []
    for d in range(BLK):
        for x in range(SIDE):
            for y in range(SIDE):
                sx, sy = (x + step, y) if axes[d % 2] == "x" else (x, y + step)
                pairs.append((d * BLK + (sx % SIDE) * SIDE + sy % SIDE, d * BLK + x * SIDE + y))
    return pairs


def turn(v, axes, step):
    return lax.ppermute(v, ("dp", "filter"), from_axis(axes, step))


def gather_near(pair):
    near = [pair] + [turn(pair, "yx", k) for k in (1, 2, 3)]
    return [jnp.stack([v[k] for v in near]) for k in range(2)]


def gather_far(nears):
    return [(own, turn(own, "xy", sign), turn(own, "xy", -sign)) for own, sign in zip(nears, (1, -1))]


def gather_last(parts):
    pieces = []
    for (own, ahead, behind), sign in zip(parts, (1, -1)):
        pieces += [own, ahead, turn(ahead, "xy", sign), behind]
    return pieces


def live_slot(s, scalars):
    return jnp.minimum(s, jnp.maximum(scalars[0] - 1, 0))


def piece_specs(count):
    return [pl.BlockSpec((SIDE, 1, BLK, CELLS), lambda s, sc: (0, live_slot(s, sc), 0, 0))] * count


def weight_specs(count):
    return [pl.BlockSpec((ROWS, C), lambda s, *_: (0, 0))] * count


def sum_spec():
    return pl.BlockSpec((C, ROWS), lambda s, *_: (0, 0))


def slot_spec():
    return pl.BlockSpec((1, BLK, CELLS), lambda s, *_: (s, 0, 0))


def pair_spec():
    return pl.BlockSpec((2, 1, BLK, CELLS), lambda s, *_: (0, s, 0, 0))


def params():
    return pltpu.CompilerParams(vmem_limit_bytes=48 * 1024 * 1024)


def cost_of(slots, convs):
    return pl.CostEstimate(
        flops=slots * convs * 2 * ROWS * C * CELLS, transcendentals=slots * BLK * CELLS, bytes_accessed=slots * convs * 2 * C * CELLS
    )


def call_one(scalars, pieces, w1):
    slots = pieces[0].shape[1]
    return pl.pallas_call(
        kernel_one,
        name="layer_one",
        grid_spec=pltpu.PrefetchScalarGridSpec(
            num_scalar_prefetch=1,
            grid=(slots,),
            in_specs=piece_specs(8) + weight_specs(1),
            out_specs=[slot_spec(), sum_spec()],
            scratch_shapes=[pltpu.VMEM((C, CELLS), jnp.bfloat16), pltpu.VMEM((ROWS, CELLS), jnp.bfloat16)],
        ),
        out_shape=[
            jax.ShapeDtypeStruct((slots, BLK, CELLS), jnp.float32),
            jax.ShapeDtypeStruct((C, ROWS), jnp.float32),
        ],
        compiler_params=params(),
        cost_estimate=cost_of(slots, 2),
    )(scalars, *pieces, w1)


def call_delta(scalars, pieces, w2t, first):
    slots = pieces[0].shape[1]
    return pl.pallas_call(
        kernel_delta,
        name="layer_one_delta",
        grid_spec=pltpu.PrefetchScalarGridSpec(
            num_scalar_prefetch=1,
            grid=(slots,),
            in_specs=piece_specs(4) + weight_specs(1) + [slot_spec()],
            out_specs=pair_spec(),
            scratch_shapes=[pltpu.VMEM((C, CELLS), jnp.bfloat16)],
        ),
        out_shape=jax.ShapeDtypeStruct((2, slots, BLK, CELLS), jnp.bfloat16),
        compiler_params=params(),
        cost_estimate=cost_of(slots, 1),
    )(scalars, *pieces, w2t, first)


def call_grads(scalars, pieces, pair, second):
    slots = pieces[0].shape[1]
    return pl.pallas_call(
        kernel_grads,
        name="weight_grads",
        grid_spec=pltpu.PrefetchScalarGridSpec(
            num_scalar_prefetch=1,
            grid=(slots,),
            in_specs=piece_specs(4) + [pair_spec(), sum_spec()],
            out_specs=[pl.BlockSpec(HALF, lambda s, *_: (0, 0, 0, 0))] * 2,
            scratch_shapes=[
                pltpu.VMEM((C, CELLS), jnp.bfloat16),
                pltpu.VMEM((ROWS, CELLS), jnp.bfloat16),
                pltpu.VMEM((C, ROWS), jnp.float32),
            ],
        ),
        out_shape=[jax.ShapeDtypeStruct(HALF, jnp.float32)] * 2,
        compiler_params=params(),
        cost_estimate=cost_of(slots, 1),
    )(scalars, *pieces, pair, second)


def call_two(scalars, pieces, w2, w1t):
    slots = pieces[0].shape[1]
    flat = jax.ShapeDtypeStruct((slots, BLK, CELLS), jnp.float32)
    return pl.pallas_call(
        kernel_two,
        name="layer_two",
        grid_spec=pltpu.PrefetchScalarGridSpec(
            num_scalar_prefetch=1,
            grid=(slots,),
            in_specs=piece_specs(8) + weight_specs(2),
            out_specs=[slot_spec(), slot_spec()],
            scratch_shapes=[
                pltpu.VMEM((C, CELLS), jnp.bfloat16),
                pltpu.VMEM((C, CELLS), jnp.bfloat16),
            ],
        ),
        out_shape=[flat, flat],
        compiler_params=params(),
        cost_estimate=pl.CostEstimate(
            flops=slots * 4 * ROWS * C * CELLS, transcendentals=0, bytes_accessed=slots * 4 * C * CELLS
        ),
    )(scalars, *pieces, w2, w1t)


def kernel_split(scalars, w1, w2, out_ref):
    lane = lax.broadcasted_iota(jnp.int32, (BLK, 128), 1) >> 4

    def split(w):
        for half in range(2):
            for low in range(0, TAPS, 8):
                taps = range(low, min(low + 8, TAPS))
                tiles = [w[t, :, half * 128:(half + 1) * 128].astype(jnp.float32) for t in taps]
                for a in range(8):
                    total = None
                    for j, tile in enumerate(tiles):
                        amount = (BLK * (j - a)) % 128
                        moved = pltpu.roll(tile, amount, 1) if amount else tile
                        total = moved if total is None else jnp.where(lane == j, moved, total)
                    width = BLK * len(tiles)
                    out_ref[half * 8 + a, :, low * BLK:low * BLK + width] = total[:, :width].astype(jnp.bfloat16)

    @pl.when(scalars[3] == 0)
    def _():
        split(w1)

    @pl.when(scalars[3] == 1)
    def _():
        split(w2)


def split_weights(scalars, w1, w2):
    whole = pl.BlockSpec((TAPS, BLK, C), lambda i, *_: (0, 0, 0))
    return pl.pallas_call(
        kernel_split,
        name="split_weights",
        grid_spec=pltpu.PrefetchScalarGridSpec(
            num_scalar_prefetch=1,
            grid=(1,),
            in_specs=[whole, whole],
            out_specs=pl.BlockSpec((BLK, BLK, ROWS), lambda i, *_: (0, 0, 0)),
        ),
        out_shape=jax.ShapeDtypeStruct((BLK, BLK, ROWS), jnp.bfloat16),
        cost_estimate=pl.CostEstimate(flops=0, transcendentals=0, bytes_accessed=4 * ROWS * C * 2),
    )(scalars, w1, w2)


def kernel_collect(mine, got, out_ref):
    lane = lax.broadcasted_iota(jnp.int32, (BLK, 128), 1) >> 4
    flipped = got[...].T
    wide = jnp.concatenate([flipped, jnp.zeros((ROWS, 128 - BLK), jnp.float32)], axis=1)
    for z in range(8):
        out_ref[z, 0] = mine[...]
    for low in range(0, TAPS, 8):
        total = None
        count = min(8, TAPS - low)
        for j in range(count):
            tile = wide[(low + j) * BLK:(low + j + 1) * BLK, :]
            moved = pltpu.roll(tile, BLK * j, 1) if j else tile
            total = moved if total is None else jnp.where(lane == j, moved, total)
        width = BLK * count
        for z in range(8):
            out_ref[z, 1, :, low * BLK:low * BLK + width] = total[:, :width]


def collect(mine, got):
    return pl.pallas_call(
        kernel_collect,
        name="collect_rows",
        out_shape=jax.ShapeDtypeStruct(HALF, jnp.float32),
        cost_estimate=pl.CostEstimate(flops=0, transcendentals=0, bytes_accessed=4 * ROWS * C),
    )(mine, got)


def kernel_finish(scalars, own, other, first_ref, second_ref, full):
    core = scalars[3]
    scale = 1.0 / (BLK * CELLS) ** 0.5
    for k, out_ref in enumerate((first_ref, second_ref)):
        for z in range(8):
            full[pl.ds(pl.multiple_of((2 * z + core) * BLK, BLK), BLK), :] = own[z, k]
            full[pl.ds(pl.multiple_of((2 * z + 1 - core) * BLK, BLK), BLK), :] = other[z, k]
        out_ref[...] = full[...].T * scale


def finish(scalars, own, other):
    half = pl.BlockSpec(HALF, lambda i, *_: (0, 0, 0, 0))
    turned = pl.BlockSpec((ROWS, C), lambda i, *_: (0, 0))
    return pl.pallas_call(
        kernel_finish,
        name="finish_gradients",
        grid_spec=pltpu.PrefetchScalarGridSpec(
            num_scalar_prefetch=1,
            grid=(1,),
            in_specs=[half, half],
            out_specs=[turned, turned],
            scratch_shapes=[pltpu.VMEM((C, ROWS), jnp.float32)],
        ),
        out_shape=[jax.ShapeDtypeStruct((ROWS, C), jnp.float32)] * 2,
        cost_estimate=pl.CostEstimate(flops=0, transcendentals=0, bytes_accessed=16 * ROWS * C),
    )(scalars, own, other)


def swap_cores(v):
    return lax.ppermute(v, "dp", [(d, d ^ 1) for d in range(BLK)])


def over_z(v):
    by_core = [[2 * z + core for z in range(8)] for core in range(2)]
    return lax.all_to_all(v, "dp", 0, 0, axis_index_groups=by_core, tiled=True)


def sum_over_dp(parts):
    mine = parts.astype(jnp.float32).sum(axis=0)
    flip = [(d * BLK + f, f * BLK + d) for d in range(BLK) for f in range(BLK)]
    got = lax.ppermute(mine[1], ("dp", "filter"), flip)
    return over_z(collect(mine[0], got))


def both_gradients(scalars, own):
    first_grad, second_grad = finish(scalars, own, swap_cores(own))
    return first_grad.reshape(TAPS, BLK, C), second_grad.reshape(TAPS, BLK, C)


def shards(patches, cotangent, first_weight, second_weight, counts):
    me = lax.axis_index("filter")
    core = lax.axis_index("dp") % 2
    scalars = jnp.stack([counts[0], me // SIDE, me % SIDE, core]).astype(jnp.int32)
    split = split_weights(scalars, first_weight, second_weight)
    nears = gather_near(jnp.stack([patches.transpose(1, 0, 2), cotangent.transpose(1, 0, 2)]))
    nears, split = lax.optimization_barrier((nears, split))
    fars = gather_far(nears)

    turned = lax.all_to_all(split, "filter", 0, 0, tiled=True).reshape(C, ROWS)
    pieces = gather_last(fars)
    w1 = first_weight.reshape(ROWS, C)
    w2 = second_weight.reshape(ROWS, C)

    first, second = call_one(scalars, pieces, w1)
    turned, first = lax.optimization_barrier((turned, first))
    other = swap_cores(turned)
    w1t = jnp.where(core == 0, turned, other).T
    w2t = jnp.where(core == 0, other, turned).T
    pair = call_delta(scalars, pieces[4:], w2t, first)
    nears = gather_near(pair)
    keep, send = call_grads(scalars, pieces[:4], pair, second)
    pair_sum = (keep + swap_cores(send)).astype(jnp.bfloat16)
    nears, pair_sum = lax.optimization_barrier((nears, pair_sum))
    fars = gather_far(nears)
    parts = over_z(pair_sum)
    fars[0], parts = lax.optimization_barrier((fars[0], parts))
    second_pieces = gather_last(fars)
    own = sum_over_dp(parts)
    out, in_grad = call_two(scalars, second_pieces, w2, w1t)
    out, in_grad, own = lax.optimization_barrier((out, in_grad, own))
    first_grad, second_grad = both_gradients(scalars, own)
    return (out.transpose(1, 0, 2), in_grad.transpose(1, 0, 2), first_grad, second_grad)


def solution(mesh):
    placed = (
        P("filter", "dp", None),
        P("filter", "dp", None),
        P(None, "filter", None),
        P(None, "filter", None),
        P("dp"),
    )
    return jax.shard_map(
        shards,
        mesh=mesh,
        in_specs=placed,
        out_specs=(
            P("filter", "dp", None),
            P("filter", "dp", None),
            P(None, "filter", None),
            P(None, "filter", None),
        ),
        check_vma=False,
    )
```

```python
import functools

import jax
import jax.numpy as jnp
from jax import lax
from jax.experimental import pallas as pl
from jax.experimental.pallas import tpu as pltpu
from jax.sharding import PartitionSpec as P

PX = 8
PY = 16
PZ = 16
CAP = 3
CELLS = 2048
PLANE = PY * PZ
C = 256
BLK = 16
TAPS = 27
ROWS = TAPS * BLK

SIDE = 4
HALF = (8, 2, BLK, ROWS)


def axis_masks():
    cell = lax.broadcasted_iota(jnp.int32, (BLK, CELLS), 1)
    pos_y = (cell >> 4) & 15
    pos_z = cell & 15
    in_y = {-1: pos_y > 0, 0: None, 1: pos_y < PY - 1}
    in_z = {-1: pos_z > 0, 0: None, 1: pos_z < PZ - 1}
    return in_y, in_z


def shift_x(v, ox):
    if ox == 0:
        return v
    zero = jnp.zeros((v.shape[0], PLANE), v.dtype)
    if ox > 0:
        return jnp.concatenate([v[:, PLANE:], zero], axis=1)
    return jnp.concatenate([zero, v[:, :-PLANE]], axis=1)


def shift_yz(v, oy, oz, masks):
    step = oy * PZ + oz
    if step == 0:
        return v
    v = pltpu.roll(v, (-step) % CELLS, 1)
    for inside in (masks[0][oy], masks[1][oz]):
        if inside is not None:
            v = jnp.where(inside, v, 0.0)
    return v


def tap_conv(w_ref, full, sign, masks):
    proj = [
        jnp.dot(w_ref[k * 9 * BLK:(k + 1) * 9 * BLK, :], full, preferred_element_type=jnp.float32)
        for k in range(3)
    ]
    total = None
    for oy in (-1, 0, 1):
        for oz in (-1, 0, 1):
            at = (3 * (oy + 1) + oz + 1) * BLK
            part = None
            for ox in (-1, 0, 1):
                term = shift_x(proj[ox + 1][at:at + BLK, :], sign * ox)
                part = term if part is None else part + term
            part = shift_yz(part, sign * oy, sign * oz, masks)
            total = part if total is None else total + part
    return total


def tap_stack(stack_ref, v, sign, masks):
    for oy in (-1, 0, 1):
        for oz in (-1, 0, 1):
            moved = shift_yz(v, sign * oy, sign * oz, masks)
            for ox in (-1, 0, 1):
                t = 9 * (ox + 1) + 3 * (oy + 1) + (oz + 1)
                stack_ref[t * BLK:(t + 1) * BLK, :] = shift_x(moved, sign * ox).astype(jnp.bfloat16)


def place(scalars, pieces, full_ref, sign):
    x, y, core = scalars[1], scalars[2], scalars[3]
    for outer in range(SIDE):
        for inner in range(SIDE):
            far, near = SIDE + sign * outer, SIDE + inner
            bx = x + jnp.where(core == 0, far, near)
            by = y + jnp.where(core == 0, near, far)
            block = lax.rem(bx, SIDE) * SIDE + lax.rem(by, SIDE)
            at = pl.multiple_of(block * BLK, BLK)
            full_ref[pl.ds(at, BLK), :] = pieces[outer][inner, 0]


def over_cells(a, b):
    return lax.dot_general(a, b, (((1,), (1,)), ((), ())), preferred_element_type=jnp.float32)


def kernel_one(scalars, *refs):
    px, gx = refs[0:4], refs[4:8]
    w1, w2t, pair_out, full_p, full_g = refs[8:]
    s = pl.program_id(0)

    @pl.when(s >= scalars[0])
    def _():
        pair_out[...] = jnp.zeros_like(pair_out)

    @pl.when(s < scalars[0])
    def _():
        masks = axis_masks()
        place(scalars, px, full_p, 1)
        place(scalars, gx, full_g, -1)
        first = tap_conv(w1, full_p[...], 1, masks)
        hidden_grad = tap_conv(w2t, full_g[...], -1, masks)
        sigma = 1.0 / (1.0 + jnp.exp(-first))
        pair_out[0, 0] = (first * sigma).astype(jnp.bfloat16)
        pair_out[1, 0] = (hidden_grad * sigma * (1.0 + first * (1.0 - sigma))).astype(jnp.bfloat16)


def kernel_grads(scalars, *refs):
    px, gx = refs[0:4], refs[4:8]
    pair, keep_out, send_out, full, stack, grads = refs[8:]
    s = pl.program_id(0)
    core = scalars[3]

    @pl.when(s == 0)
    def _():
        grads[...] = jnp.zeros_like(grads)

    @pl.when(s < scalars[0])
    def _():
        masks = axis_masks()
        place(scalars, px, full, 1)
        tap_stack(stack, pair[1, 0].astype(jnp.float32), -1, masks)
        grads[0] += over_cells(full[...], stack[...])
        place(scalars, gx, full, -1)
        tap_stack(stack, pair[0, 0].astype(jnp.float32), 1, masks)
        grads[1] += over_cells(full[...], stack[...])

    @pl.when(s == pl.num_programs(0) - 1)
    def _():
        for z in range(8):
            for k in range(2):
                keep_out[z, k] = grads[k, pl.ds(pl.multiple_of((2 * z + core) * BLK, BLK), BLK), :]
                send_out[z, k] = grads[k, pl.ds(pl.multiple_of((2 * z + 1 - core) * BLK, BLK), BLK), :]


def kernel_two(scalars, *refs):
    hx, dx = refs[0:4], refs[4:8]
    w2, w1t, out_ref, in_ref, full_h, full_d = refs[8:]
    s = pl.program_id(0)

    @pl.when(s >= scalars[0])
    def _():
        out_ref[...] = jnp.zeros_like(out_ref)
        in_ref[...] = jnp.zeros_like(in_ref)

    @pl.when(s < scalars[0])
    def _():
        masks = axis_masks()
        place(scalars, hx, full_h, 1)
        place(scalars, dx, full_d, -1)
        out_ref[0] = tap_conv(w2, full_h[...], 1, masks)
        in_ref[0] = tap_conv(w1t, full_d[...], -1, masks)


def from_axis(axes, step):
    pairs = []
    for d in range(BLK):
        for x in range(SIDE):
            for y in range(SIDE):
                sx, sy = (x + step, y) if axes[d % 2] == "x" else (x, y + step)
                pairs.append((d * BLK + (sx % SIDE) * SIDE + sy % SIDE, d * BLK + x * SIDE + y))
    return pairs


def turn(v, axes, step):
    return lax.ppermute(v, ("dp", "filter"), from_axis(axes, step))


def gather_near(pair):
    near = [pair] + [turn(pair, "yx", k) for k in (1, 2, 3)]
    return [jnp.stack([v[k] for v in near]) for k in range(2)]


def gather_far(nears):
    return [(own, turn(own, "xy", sign), turn(own, "xy", -sign)) for own, sign in zip(nears, (1, -1))]


def gather_last(parts):
    pieces = []
    for (own, ahead, behind), sign in zip(parts, (1, -1)):
        pieces += [own, ahead, turn(ahead, "xy", sign), behind]
    return pieces


def live_slot(s, scalars):
    return jnp.minimum(s, jnp.maximum(scalars[0] - 1, 0))


def piece_specs():
    return [pl.BlockSpec((SIDE, 1, BLK, CELLS), lambda s, sc: (0, live_slot(s, sc), 0, 0))] * 8


def weight_specs():
    return [pl.BlockSpec((ROWS, C), lambda s, *_: (0, 0))] * 2


def slot_spec():
    return pl.BlockSpec((1, BLK, CELLS), lambda s, *_: (s, 0, 0))


def pair_spec():
    return pl.BlockSpec((2, 1, BLK, CELLS), lambda s, *_: (0, s, 0, 0))


def params():
    return pltpu.CompilerParams(vmem_limit_bytes=48 * 1024 * 1024)


def call_one(scalars, pieces, w1, w2t):
    slots = pieces[0].shape[1]
    pair = jax.ShapeDtypeStruct((2, slots, BLK, CELLS), jnp.bfloat16)
    return pl.pallas_call(
        kernel_one,
        name="layer_one",
        grid_spec=pltpu.PrefetchScalarGridSpec(
            num_scalar_prefetch=1,
            grid=(slots,),
            in_specs=piece_specs() + weight_specs(),
            out_specs=pair_spec(),
            scratch_shapes=[pltpu.VMEM((C, CELLS), jnp.bfloat16)] * 2,
        ),
        out_shape=pair,
        compiler_params=params(),
        cost_estimate=pl.CostEstimate(
            flops=slots * 4 * ROWS * C * CELLS, transcendentals=slots * BLK * CELLS, bytes_accessed=slots * 4 * C * CELLS
        ),
    )(scalars, *pieces, w1, w2t)


def call_grads(scalars, pieces, pair):
    slots = pieces[0].shape[1]
    return pl.pallas_call(
        kernel_grads,
        name="weight_grads",
        grid_spec=pltpu.PrefetchScalarGridSpec(
            num_scalar_prefetch=1,
            grid=(slots,),
            in_specs=piece_specs() + [pair_spec()],
            out_specs=[pl.BlockSpec(HALF, lambda s, *_: (0, 0, 0, 0))] * 2,
            scratch_shapes=[
                pltpu.VMEM((C, CELLS), jnp.bfloat16),
                pltpu.VMEM((ROWS, CELLS), jnp.bfloat16),
                pltpu.VMEM((2, C, ROWS), jnp.float32),
            ],
        ),
        out_shape=[jax.ShapeDtypeStruct(HALF, jnp.float32)] * 2,
        compiler_params=params(),
        cost_estimate=pl.CostEstimate(
            flops=slots * 4 * ROWS * C * CELLS, transcendentals=0, bytes_accessed=slots * 4 * C * CELLS
        ),
    )(scalars, *pieces, pair)


def call_two(scalars, pieces, w2, w1t):
    slots = pieces[0].shape[1]
    flat = jax.ShapeDtypeStruct((slots, BLK, CELLS), jnp.float32)
    return pl.pallas_call(
        kernel_two,
        name="layer_two",
        grid_spec=pltpu.PrefetchScalarGridSpec(
            num_scalar_prefetch=1,
            grid=(slots,),
            in_specs=piece_specs() + weight_specs(),
            out_specs=[slot_spec(), slot_spec()],
            scratch_shapes=[
                pltpu.VMEM((C, CELLS), jnp.bfloat16),
                pltpu.VMEM((C, CELLS), jnp.bfloat16),
            ],
        ),
        out_shape=[flat, flat],
        compiler_params=params(),
        cost_estimate=pl.CostEstimate(
            flops=slots * 4 * ROWS * C * CELLS, transcendentals=0, bytes_accessed=slots * 4 * C * CELLS
        ),
    )(scalars, *pieces, w2, w1t)


def kernel_split(scalars, w1, w2, out_ref):
    lane = lax.broadcasted_iota(jnp.int32, (BLK, 128), 1) >> 4

    def split(w):
        for half in range(2):
            for low in range(0, TAPS, 8):
                taps = range(low, min(low + 8, TAPS))
                tiles = [w[t, :, half * 128:(half + 1) * 128].astype(jnp.float32) for t in taps]
                for a in range(8):
                    total = None
                    for j, tile in enumerate(tiles):
                        amount = (BLK * (j - a)) % 128
                        moved = pltpu.roll(tile, amount, 1) if amount else tile
                        total = moved if total is None else jnp.where(lane == j, moved, total)
                    width = BLK * len(tiles)
                    out_ref[half * 8 + a, :, low * BLK:low * BLK + width] = total[:, :width].astype(jnp.bfloat16)

    @pl.when(scalars[3] == 0)
    def _():
        split(w1)

    @pl.when(scalars[3] == 1)
    def _():
        split(w2)


def split_weights(scalars, w1, w2):
    whole = pl.BlockSpec((TAPS, BLK, C), lambda i, *_: (0, 0, 0))
    return pl.pallas_call(
        kernel_split,
        name="split_weights",
        grid_spec=pltpu.PrefetchScalarGridSpec(
            num_scalar_prefetch=1,
            grid=(1,),
            in_specs=[whole, whole],
            out_specs=pl.BlockSpec((BLK, BLK, ROWS), lambda i, *_: (0, 0, 0)),
        ),
        out_shape=jax.ShapeDtypeStruct((BLK, BLK, ROWS), jnp.bfloat16),
        cost_estimate=pl.CostEstimate(flops=0, transcendentals=0, bytes_accessed=4 * ROWS * C * 2),
    )(scalars, w1, w2)


def kernel_collect(mine, got, out_ref):
    lane = lax.broadcasted_iota(jnp.int32, (BLK, 128), 1) >> 4
    flipped = got[...].T
    wide = jnp.concatenate([flipped, jnp.zeros((ROWS, 128 - BLK), jnp.float32)], axis=1)
    for z in range(8):
        out_ref[z, 0] = mine[...]
    for low in range(0, TAPS, 8):
        total = None
        count = min(8, TAPS - low)
        for j in range(count):
            tile = wide[(low + j) * BLK:(low + j + 1) * BLK, :]
            moved = pltpu.roll(tile, BLK * j, 1) if j else tile
            total = moved if total is None else jnp.where(lane == j, moved, total)
        width = BLK * count
        for z in range(8):
            out_ref[z, 1, :, low * BLK:low * BLK + width] = total[:, :width]


def collect(mine, got):
    return pl.pallas_call(
        kernel_collect,
        name="collect_rows",
        out_shape=jax.ShapeDtypeStruct(HALF, jnp.float32),
        cost_estimate=pl.CostEstimate(flops=0, transcendentals=0, bytes_accessed=4 * ROWS * C),
    )(mine, got)


def kernel_finish(scalars, own, other, first_ref, second_ref, full):
    core = scalars[3]
    scale = 1.0 / (BLK * CELLS) ** 0.5
    for k, out_ref in enumerate((first_ref, second_ref)):
        for z in range(8):
            full[pl.ds(pl.multiple_of((2 * z + core) * BLK, BLK), BLK), :] = own[z, k]
            full[pl.ds(pl.multiple_of((2 * z + 1 - core) * BLK, BLK), BLK), :] = other[z, k]
        out_ref[...] = full[...].T * scale


def finish(scalars, own, other):
    half = pl.BlockSpec(HALF, lambda i, *_: (0, 0, 0, 0))
    turned = pl.BlockSpec((ROWS, C), lambda i, *_: (0, 0))
    return pl.pallas_call(
        kernel_finish,
        name="finish_gradients",
        grid_spec=pltpu.PrefetchScalarGridSpec(
            num_scalar_prefetch=1,
            grid=(1,),
            in_specs=[half, half],
            out_specs=[turned, turned],
            scratch_shapes=[pltpu.VMEM((C, ROWS), jnp.float32)],
        ),
        out_shape=[jax.ShapeDtypeStruct((ROWS, C), jnp.float32)] * 2,
        cost_estimate=pl.CostEstimate(flops=0, transcendentals=0, bytes_accessed=16 * ROWS * C),
    )(scalars, own, other)


def swap_cores(v):
    return lax.ppermute(v, "dp", [(d, d ^ 1) for d in range(BLK)])


def over_z(v):
    by_core = [[2 * z + core for z in range(8)] for core in range(2)]
    return lax.all_to_all(v, "dp", 0, 0, axis_index_groups=by_core, tiled=True)


def reduce_rows(parts):
    mine = parts.astype(jnp.float32).sum(axis=0)
    flip = [(d * BLK + f, f * BLK + d) for d in range(BLK) for f in range(BLK)]
    return mine[0], lax.ppermute(mine[1], ("dp", "filter"), flip)


def both_gradients(scalars, own):
    first_grad, second_grad = finish(scalars, own, swap_cores(own))
    return first_grad.reshape(TAPS, BLK, C), second_grad.reshape(TAPS, BLK, C)


def shards(patches, cotangent, first_weight, second_weight, counts):
    me = lax.axis_index("filter")
    core = lax.axis_index("dp") % 2
    scalars = jnp.stack([counts[0], me // SIDE, me % SIDE, core]).astype(jnp.int32)
    split = split_weights(scalars, first_weight, second_weight)
    nears = gather_near(jnp.stack([patches.transpose(1, 0, 2), cotangent.transpose(1, 0, 2)]))
    nears, split = lax.optimization_barrier((nears, split))
    fars = gather_far(nears)

    turned = lax.all_to_all(split, "filter", 0, 0, tiled=True).reshape(C, ROWS)
    pieces = gather_last(fars)
    other = swap_cores(turned)
    w1t = jnp.where(core == 0, turned, other).T
    w2t = jnp.where(core == 0, other, turned).T
    w1 = first_weight.reshape(ROWS, C)
    w2 = second_weight.reshape(ROWS, C)

    pair = call_one(scalars, pieces, w1, w2t)
    nears = gather_near(pair)
    keep, send = call_grads(scalars, pieces, pair)
    pair_sum = (keep + swap_cores(send)).astype(jnp.bfloat16)
    parts = over_z(pair_sum)
    last, parts = lax.optimization_barrier((nears[1], parts))
    fars = gather_far([nears[0], last])
    mine, got = reduce_rows(parts)
    last, got = lax.optimization_barrier((fars[1], got))
    second_pieces = gather_last([fars[0], last])
    own = over_z(collect(mine, got))
    out, in_grad = call_two(scalars, second_pieces, w2, w1t)
    out, in_grad, own = lax.optimization_barrier((out, in_grad, own))
    first_grad, second_grad = both_gradients(scalars, own)
    return (out.transpose(1, 0, 2), in_grad.transpose(1, 0, 2), first_grad, second_grad)


def solution(mesh):
    placed = (
        P("filter", "dp", None),
        P("filter", "dp", None),
        P(None, "filter", None),
        P(None, "filter", None),
        P("dp"),
    )
    return jax.shard_map(
        shards,
        mesh=mesh,
        in_specs=placed,
        out_specs=(
            P("filter", "dp", None),
            P("filter", "dp", None),
            P(None, "filter", None),
            P(None, "filter", None),
        ),
        check_vma=False,
    )
```
